256 devices in a mesh: dp: 4 (over x_hi, core), ctx: 64 (over z, y, x_lo).
Axes of the slice: x: 4 (x_hi: 2, x_lo: 2; x = x_hi * 2 + x_lo), y: 4, z: 8, core: 2. Of those that a mesh axis runs over, the one named last changes fastest.
Arguments:
- queries: bfloat16 [4, 8192, 2560], P('dp', 'ctx'), may hold values from -6 to 6
- keys: bfloat16 [4, 8192, 512], P('dp', 'ctx'), may hold values from -6 to 6
- values: bfloat16 [4, 8192, 512], P('dp', 'ctx'), may hold values from -6 to 6
- out_grad: bfloat16 [4, 8192, 2560], P('dp', 'ctx'), may hold values from -24 to 24
- layer_input: bfloat16 [4, 8192, 5120], P('dp', 'ctx'), may hold values from -16 to 16
- doc_lens: int32 [4, 16], P('dp'), may hold values from 1 to 1024, 8192 in all within a row
Outputs:
- attn_out: bfloat16 [4, 8192, 2560], P('dp', 'ctx')
- query_grad: bfloat16 [4, 8192, 2560], P('dp', 'ctx')
- key_grad: bfloat16 [4, 8192, 512], P('dp', 'ctx')
- value_grad: bfloat16 [4, 8192, 512], P('dp', 'ctx')
- weight_grad: float32 [5120, 1024], P(('dp', 'ctx'))
The draws below stay inside these ranges and needn't reach their ends.
Inputs may be any that keep to these rules, and one draw needn't show every extreme that they name: `doc_lens`: the documents of a micro-batch lie end to end and fill its 8192 positions; in every micro-batch the longest has exactly 1024 positions.
All inputs are finite; a program needn't handle non-finite values.
Results may differ from the reference program's by a relative error of at most 0.029.
Values may be sent and summed in bfloat16 or wider, within the bound.
No kernel may reach another device: no remote copies, remote signals or barrier semaphores. Data moves between devices by JAX's collectives and lax.ppermute only.
A program may use at most 128 MiB of HBM per device.

```python
import math
import jax
import jax.numpy as jnp
import numpy as np
from jax import lax

D = 5120
HQ = 20
HK = 4
HD = 128
TOK_DEV = 128
NDOC = 16
REACH = 8
MOST = 1024
SEQ = 8192
MB = 4


def draw_queries(key, part):
    drawn = jnp.clip(jax.random.normal(jax.random.fold_in(key, 1), (MB, SEQ, HQ * HD), jnp.float32), -6.0, 6.0)
    return drawn.astype(jnp.bfloat16)


def draw_keys(key, part):
    drawn = jnp.clip(jax.random.normal(jax.random.fold_in(key, 2), (MB, SEQ, HK * HD), jnp.float32), -6.0, 6.0)
    return drawn.astype(jnp.bfloat16)


def strengthened(values, key, source, target, parts, factor):
    owner, partner = [(jnp.arange(values.shape[position]) // (values.shape[position] // parts)).reshape([-1 if axis == position else 1 for axis in range(values.ndim)]) for position in (source, target)]
    chosen = jax.random.permutation(key, parts)[partner]
    strong = (owner == chosen) | (owner == (partner + parts // 2) % parts)
    return jnp.where(strong, factor * values, values)


def block_levels(own_key, shape, pieces, smallest, top_value):
    def one(position, parts):
        draws = jax.random.uniform(jax.random.fold_in(jax.random.fold_in(own_key, 6), position), (parts,), jnp.float32, smallest / len(pieces), top_value / len(pieces))
        return jnp.repeat(jnp.exp(draws), shape[position] // parts).reshape((-1,) + (1,) * (len(shape) - position - 1))

    gain = one(*pieces[0])
    for cut in pieces[1:]:
        gain = gain * one(*cut)
    return gain


def length_profile(number_of, total, limit, lean):
    portions = [(1 << 20) // math.isqrt(rank ** lean) + 1 for rank in range(2, number_of + 1)]
    surplus, given = total - limit - (number_of - 1), [1] * (number_of - 1)
    while surplus > 0:
        candidates = [i for i in range(number_of - 1) if given[i] < limit]
        mass, remaining = sum([portions[i] for i in candidates]), surplus
        for i in candidates:
            extra = min(limit - given[i], max(1, remaining * portions[i] // mass), surplus)
            given[i] = given[i] + extra
            surplus = surplus - extra
    return np.array([limit] + given)


def uneven(rng, number_of, total, limit, slope):
    if number_of == 2:
        one = jax.random.randint(rng, (), max(1, total - limit), min(limit, total - 1) + 1)
        return jnp.stack([one, total - one])
    tallies = jnp.asarray(length_profile(number_of, total, limit, slope), jnp.int32)
    twos = (number_of - 1) // 2
    giver, receiver = tallies[1:1 + 2 * twos:2], tallies[2:2 + 2 * twos:2]
    room = jnp.minimum(giver - 1, limit - receiver)
    shifted = jax.random.randint(jax.random.fold_in(rng, 1), (twos,), 0, 1 << 20) % (room + 1)
    tallies = tallies.at[1:1 + 2 * twos:2].set(giver - shifted).at[2:2 + 2 * twos:2].set(receiver + shifted)
    return tallies[jax.random.permutation(jax.random.fold_in(rng, 2), number_of)]


def bell_draw(rng, shape, deviation, reach, shards=(), held_as=jnp.bfloat16):
    loudness = block_levels(rng, shape, shards, -0.22, 0.18) if shards else 1.0
    drawn = jax.random.normal(rng, shape, jnp.float32) * deviation * loudness
    return jnp.minimum(jnp.maximum(drawn, -reach), reach).astype(held_as)


def gaussian_with(key, shape, scale, reach, cuts, heavy, kind=jnp.bfloat16):
    entries = scale * jax.random.normal(key, shape, jnp.float32)
    if cuts:
        entries = entries * block_levels(key, shape, cuts, -0.22, 0.18)
    return jnp.clip(strengthened(entries, jax.random.fold_in(key, 3), *heavy), -reach, reach).astype(kind)


def setup_inputs(seed: int = 0) -> dict:
    splits = jax.random.split(jax.random.key(seed), 7)
    queries = draw_queries(jax.random.fold_in(splits[6], 71), 0)
    keys = draw_keys(jax.random.fold_in(splits[6], 71), 0)
    values = bell_draw(splits[2], (MB, SEQ, HK * HD), 1.0, 6.0, ((0, 4), (1, 64)))
    out_grad = bell_draw(splits[3], (MB, SEQ, HQ * HD), 4.0, 24.0, ((0, 4), (1, 64)))
    layer_input = gaussian_with(splits[4], (MB, SEQ, D), 1.0, 16.0, ((0, 4), (1, 64)), (1, 2, 64, 4.0))
    doc_lens = jax.vmap(lambda own: uneven(own, NDOC, SEQ, MOST, 2))(jax.random.split(splits[5], MB)).reshape((MB, NDOC)).astype(jnp.int32)
    return dict(queries=queries, keys=keys, values=values, out_grad=out_grad, layer_input=layer_input, doc_lens=doc_lens)


NEGATIVE = -1e+30

def doc_index(lengths_row, positions):
    bounds = jnp.cumsum(lengths_row.astype(jnp.int32))
    return lax.optimization_barrier(jnp.sum((positions[:, None] >= bounds[None, :]).astype(jnp.int32), axis=1))

def one_batch(query_seq, key_seq, value_seq, grad_seq, lengths_row):
    group = HQ // HK
    inverse = 1.0 / math.sqrt(HD)
    margin = REACH * TOK_DEV
    window = (REACH + 1) * TOK_DEV
    blocks = SEQ // TOK_DEV
    positions = jnp.arange(SEQ, dtype=jnp.int32)
    doc_ids = doc_index(lengths_row, positions)
    pad_pos = jnp.arange(-margin, SEQ, dtype=jnp.int32)
    pad_ids = jnp.concatenate([jnp.full((margin,), -1, jnp.int32), doc_ids])
    zero_rows = jnp.zeros((margin, HK * HD), key_seq.dtype)
    key_pad = jnp.concatenate([zero_rows, key_seq], axis=0)
    value_pad = jnp.concatenate([zero_rows, value_seq], axis=0)

    def block_step(carry, index):
        key_acc, value_acc = carry
        start = (index * TOK_DEV).astype(jnp.int32)
        query_blk = lax.dynamic_slice_in_dim(query_seq, start, TOK_DEV, 0).astype(jnp.float32).reshape(TOK_DEV, HK, group, HD)
        grad_blk = lax.dynamic_slice_in_dim(grad_seq, start, TOK_DEV, 0).astype(jnp.float32).reshape(TOK_DEV, HK, group, HD)
        key_win = lax.dynamic_slice_in_dim(key_pad, start, window, 0).astype(jnp.float32).reshape(window, HK, HD)
        value_win = lax.dynamic_slice_in_dim(value_pad, start, window, 0).astype(jnp.float32).reshape(window, HK, HD)
        query_pos = lax.dynamic_slice_in_dim(positions, start, TOK_DEV, 0)
        query_ids = lax.dynamic_slice_in_dim(doc_ids, start, TOK_DEV, 0)
        key_pos = lax.dynamic_slice_in_dim(pad_pos, start, window, 0)
        key_ids = lax.dynamic_slice_in_dim(pad_ids, start, window, 0)
        allowed = (key_pos[None, :] <= query_pos[:, None]) & (key_ids[None, :] == query_ids[:, None]) & (key_pos[None, :] >= 0)
        scores = jnp.einsum('ighd,jgd->ghij', query_blk, key_win) * inverse
        scores = jnp.where(allowed[None, None], scores, NEGATIVE)
        peak = lax.optimization_barrier(jnp.max(scores, axis=-1, keepdims=True))
        exponent = jnp.exp(scores - peak)
        probs = exponent / lax.optimization_barrier(jnp.sum(exponent, axis=-1, keepdims=True))
        probs_half = lax.optimization_barrier(probs.astype(jnp.bfloat16)).astype(jnp.float32)
        output = jnp.einsum('ghij,jgd->ighd', probs_half, value_win)
        out_half = output.astype(jnp.bfloat16)
        out_back = lax.optimization_barrier(out_half).astype(jnp.float32)
        delta = jnp.einsum('ighd,ighd->ghi', grad_blk, out_back)
        prob_grad = jnp.einsum('ighd,jgd->ghij', grad_blk, value_win)
        score_grad = lax.optimization_barrier((probs * (prob_grad - delta[..., None])).astype(jnp.bfloat16)).astype(jnp.float32)
        query_part = (jnp.einsum('ghij,jgd->ighd', score_grad, key_win) * inverse).astype(jnp.bfloat16)
        key_part = jnp.einsum('ghij,ighd->jgd', score_grad, query_blk) * inverse
        value_part = jnp.einsum('ghij,ighd->jgd', probs_half, grad_blk)
        key_acc = lax.dynamic_update_slice_in_dim(key_acc, lax.dynamic_slice_in_dim(key_acc, start, window, 0) + key_part.reshape(window, HK * HD), start, 0)
        value_acc = lax.dynamic_update_slice_in_dim(value_acc, lax.dynamic_slice_in_dim(value_acc, start, window, 0) + value_part.reshape(window, HK * HD), start, 0)
        return ((key_acc, value_acc), (out_half.reshape(TOK_DEV, HQ * HD), query_part.reshape(TOK_DEV, HQ * HD)))
    empty = jnp.zeros((margin + SEQ, HK * HD), jnp.float32)
    (key_acc, value_acc), (outputs, query_grads) = lax.scan(block_step, (empty, empty), jnp.arange(blocks, dtype=jnp.int32))
    return (outputs.reshape(SEQ, HQ * HD), query_grads.reshape(SEQ, HQ * HD), key_acc[margin:].astype(jnp.bfloat16), value_acc[margin:].astype(jnp.bfloat16))

def reference(queries, keys, values, out_grad, layer_input, doc_lens):
    attn_list, query_list, key_list, value_list = ([], [], [], [])
    grad_total = jnp.zeros((D, 2 * HK * HD), jnp.float32)
    for batch in range(MB):
        attn_part, query_part, key_part, value_part = one_batch(queries[batch], keys[batch], values[batch], out_grad[batch], doc_lens[batch])
        attn_list.append(attn_part)
        query_list.append(query_part)
        key_list.append(key_part)
        value_list.append(value_part)
        joined = jnp.concatenate([key_part, value_part], axis=1)
        grad_total = grad_total + jnp.dot(layer_input[batch].T, joined, preferred_element_type=jnp.float32)
    weight_grad = grad_total / math.sqrt(MB * SEQ)
    return (jnp.stack(attn_list), jnp.stack(query_list), jnp.stack(key_list), jnp.stack(value_list), weight_grad)
```

```python
import math

import jax
import jax.numpy as jnp
from jax import lax
from jax.sharding import Mesh
from jax.sharding import PartitionSpec as P

D = 5120
HD = 128


NEGATIVE = -1e30
CTX = ("cz", "cw")


def shifted(block, distance, n_ctx):
    route = [(i - distance, i) for i in range(n_ctx) if 0 <= i - distance < n_ctx]
    return lax.ppermute(block, CTX, route)


def doc_index(lengths_row, positions):
    bounds = jnp.cumsum(lengths_row)
    return jnp.sum((positions[:, None] >= bounds[None, :]).astype(jnp.int32), axis=1)


def make_shards(n_data, n_cz, n_cw):
    n_context = n_cz * n_cw

    def shards(queries, keys, values, out_grad, layer_input, doc_lens):
        tok_rows = queries.shape[1]
        kv_width = keys.shape[2]
        heads_kv = kv_width // HD
        group = queries.shape[2] // kv_width
        inverse = 1.0 / math.sqrt(HD)
        blocks_back = min(8, n_context // 4)

        owned = D // (n_data * n_context)
        token_rows = layer_input[0].reshape(tok_rows, n_data, n_cz, n_cw, owned)
        column_share = lax.all_to_all(token_rows, "cw", split_axis=3, concat_axis=0, tiled=True)
        column_share = column_share.reshape(tok_rows * n_cw, n_data * n_cz * owned)

        own_pair = jnp.concatenate([keys[0], values[0]], axis=1)
        earlier = [shifted(own_pair, d, n_context) for d in range(blocks_back, 0, -1)]
        window_pair = jnp.concatenate(earlier + [own_pair], axis=0)
        span = window_pair.shape[0]
        key_win = window_pair[:, :kv_width].reshape(span, heads_kv, HD)
        value_win = window_pair[:, kv_width:].reshape(span, heads_kv, HD)
        device = lax.axis_index("cz") * n_cw + lax.axis_index("cw")
        query_pos = device * tok_rows + jnp.arange(tok_rows, dtype=jnp.int32)
        key_pos = (device - blocks_back) * tok_rows + jnp.arange(span, dtype=jnp.int32)
        query_ids = doc_index(doc_lens[0], query_pos)
        key_ids = doc_index(doc_lens[0], key_pos)
        allowed = (
            (key_pos[None, :] <= query_pos[:, None])
            & (key_ids[None, :] == query_ids[:, None])
            & (key_pos[None, :] >= 0)
        )
        query_blk = queries[0].reshape(tok_rows, heads_kv, group, HD)
        grad_blk = out_grad[0].reshape(tok_rows, heads_kv, group, HD)
        scores = (
            jnp.einsum("ighd,jgd->ghij", query_blk, key_win, preferred_element_type=jnp.float32)
            * inverse
        )
        scores = jnp.where(allowed[None, None], scores, NEGATIVE)
        peak = jnp.max(scores, axis=-1, keepdims=True)
        exponent = jnp.exp(scores - peak)
        probs = exponent / jnp.sum(exponent, axis=-1, keepdims=True)
        probs_half = probs.astype(jnp.bfloat16)
        output = jnp.einsum("ghij,jgd->ighd", probs_half, value_win, preferred_element_type=jnp.float32)
        out_half = output.astype(jnp.bfloat16)
        delta = jnp.einsum("ighd,ighd->ghi", grad_blk, out_half, preferred_element_type=jnp.float32)
        prob_grad = jnp.einsum(
            "ighd,jgd->ghij", grad_blk, value_win, preferred_element_type=jnp.float32
        )
        score_grad = (probs * (prob_grad - delta[..., None])).astype(jnp.bfloat16)
        query_part = (
            jnp.einsum("ghij,jgd->ighd", score_grad, key_win, preferred_element_type=jnp.float32)
            * inverse
        ).astype(jnp.bfloat16)
        key_part = (
            jnp.einsum("ghij,ighd->jgd", score_grad, query_blk, preferred_element_type=jnp.float32)
            * inverse
        )
        value_part = jnp.einsum(
            "ghij,ighd->jgd", probs_half, grad_blk, preferred_element_type=jnp.float32
        )
        pair_grad = jnp.concatenate(
            [key_part.reshape(span, kv_width), value_part.reshape(span, kv_width)], axis=1
        )

        def block_back(distance):
            first_row = (blocks_back - distance) * tok_rows
            return pair_grad[first_row : first_row + tok_rows]

        total = block_back(0)
        for distance in range(1, blocks_back + 1):
            total = total + shifted(block_back(distance), -distance, n_context)
        pair_half = total.astype(jnp.bfloat16)

        grad_scale = 1.0 / math.sqrt(tok_rows * n_context * n_data)
        group_grad = lax.all_gather(pair_half, "cw", axis=0, tiled=True)
        batch_grad = lax.dot_general(
            column_share,
            group_grad,
            (((0,), (0,)), ((), ())),
            preferred_element_type=jnp.float32,
        )
        weight_grad = lax.psum_scatter(
            batch_grad * grad_scale, ("dp", "cz"), scatter_dimension=0, tiled=True
        )
        attn_out = out_half.reshape(tok_rows, group * kv_width)[None]
        query_grad = query_part.reshape(tok_rows, group * kv_width)[None]
        key_grad = pair_half[:, :kv_width][None]
        value_grad = pair_half[:, kv_width:][None]
        return (attn_out, query_grad, key_grad, value_grad, weight_grad)

    return shards


def solution(mesh):
    n_data = mesh.shape["dp"]
    n_context = mesh.shape["ctx"]
    n_cw = 8 if n_context % 8 == 0 else n_context
    n_cz = n_context // n_cw
    split = Mesh(mesh.devices.reshape(n_data, n_cz, n_cw), ("dp", "cz", "cw"))
    tokens = P("dp", CTX, None)
    in_specs = (tokens, tokens, tokens, tokens, tokens, P("dp", None))
    out_specs = (tokens, tokens, tokens, tokens, P(("dp", "cz", "cw"), None))
    return jax.shard_map(
        make_shards(n_data, n_cz, n_cw),
        mesh=split,
        in_specs=in_specs,
        out_specs=out_specs,
        check_vma=False,
    )
```

```python
import math

import jax
import jax.numpy as jnp
from jax import lax
from jax.sharding import Mesh
from jax.sharding import PartitionSpec as P

D = 5120
HD = 128


NEGATIVE = -1e30
CTX = ("cz", "cw")


def shifted(block, distance, n_ctx):
    route = [(i - distance, i) for i in range(n_ctx) if 0 <= i - distance < n_ctx]
    return lax.ppermute(block, CTX, route)


def doc_index(lengths_row, positions):
    bounds = jnp.cumsum(lengths_row)
    return jnp.sum((positions[:, None] >= bounds[None, :]).astype(jnp.int32), axis=1)


def make_shards(n_data, n_cz, n_cw):
    n_context = n_cz * n_cw

    def shards(queries, keys, values, out_grad, layer_input, doc_lens):
        tok_rows = queries.shape[1]
        kv_width = keys.shape[2]
        heads_kv = kv_width // HD
        group = queries.shape[2] // kv_width
        inverse = 1.0 / math.sqrt(HD)
        blocks_back = min(8, n_context // 4)

        owned = D // (n_data * n_context)
        member = lax.axis_index("cw")
        chunks = layer_input[0].reshape(tok_rows, n_data, n_cz, n_cw, owned)
        chunks = chunks.transpose(3, 0, 2, 1, 4).reshape(n_cw, tok_rows, n_cz * n_data * owned)
        received = [lax.dynamic_index_in_dim(chunks, member, 0, keepdims=False)]
        for k in range(1, n_cw):
            route = [(i, (i + k) % n_cw) for i in range(n_cw)]
            outgoing = lax.dynamic_index_in_dim(chunks, (member + k) % n_cw, 0, keepdims=False)
            received.append(lax.ppermute(outgoing, "cw", route))
        column_share = jnp.concatenate(received[::-1], axis=0)

        own_pair = jnp.concatenate([keys[0], values[0]], axis=1)
        earlier = [shifted(own_pair, d, n_context) for d in range(blocks_back, 0, -1)]
        window_pair = jnp.concatenate(earlier + [own_pair], axis=0)
        span = window_pair.shape[0]
        key_win = window_pair[:, :kv_width].reshape(span, heads_kv, HD)
        value_win = window_pair[:, kv_width:].reshape(span, heads_kv, HD)
        device = lax.axis_index("cz") * n_cw + lax.axis_index("cw")
        query_pos = device * tok_rows + jnp.arange(tok_rows, dtype=jnp.int32)
        key_pos = (device - blocks_back) * tok_rows + jnp.arange(span, dtype=jnp.int32)
        query_ids = doc_index(doc_lens[0], query_pos)
        key_ids = doc_index(doc_lens[0], key_pos)
        allowed = (
            (key_pos[None, :] <= query_pos[:, None])
            & (key_ids[None, :] == query_ids[:, None])
            & (key_pos[None, :] >= 0)
        )
        query_blk = queries[0].reshape(tok_rows, heads_kv, group, HD)
        grad_blk = out_grad[0].reshape(tok_rows, heads_kv, group, HD)
        scores = (
            jnp.einsum("ighd,jgd->ghij", query_blk, key_win, preferred_element_type=jnp.float32)
            * inverse
        )
        scores = jnp.where(allowed[None, None], scores, NEGATIVE)
        peak = jnp.max(scores, axis=-1, keepdims=True)
        exponent = jnp.exp(scores - peak)
        probs = exponent / jnp.sum(exponent, axis=-1, keepdims=True)
        probs_half = probs.astype(jnp.bfloat16)
        output = jnp.einsum("ghij,jgd->ighd", probs_half, value_win, preferred_element_type=jnp.float32)
        out_half = output.astype(jnp.bfloat16)
        delta = jnp.einsum("ighd,ighd->ghi", grad_blk, out_half, preferred_element_type=jnp.float32)
        prob_grad = jnp.einsum(
            "ighd,jgd->ghij", grad_blk, value_win, preferred_element_type=jnp.float32
        )
        score_grad = (probs * (prob_grad - delta[..., None])).astype(jnp.bfloat16)
        query_part = (
            jnp.einsum("ghij,jgd->ighd", score_grad, key_win, preferred_element_type=jnp.float32)
            * inverse
        ).astype(jnp.bfloat16)
        key_part = (
            jnp.einsum("ghij,ighd->jgd", score_grad, query_blk, preferred_element_type=jnp.float32)
            * inverse
        )
        value_part = jnp.einsum(
            "ghij,ighd->jgd", probs_half, grad_blk, preferred_element_type=jnp.float32
        )
        pair_grad = jnp.concatenate(
            [key_part.reshape(span, kv_width), value_part.reshape(span, kv_width)], axis=1
        )

        def block_back(distance):
            first_row = (blocks_back - distance) * tok_rows
            return pair_grad[first_row : first_row + tok_rows]

        total = block_back(0)
        for distance in range(1, blocks_back + 1):
            total = total + shifted(block_back(distance), -distance, n_context)
        pair_half = total.astype(jnp.bfloat16)

        grad_scale = 1.0 / math.sqrt(tok_rows * n_context * n_data)
        group_grad = lax.all_gather(pair_half, "cw", axis=0, tiled=True)
        group_grad = lax.dynamic_slice_in_dim(
            jnp.concatenate([group_grad, group_grad], axis=0),
            ((member + 1) % n_cw) * tok_rows,
            n_cw * tok_rows,
            0,
        )
        batch_grad = lax.dot_general(
            column_share,
            group_grad,
            (((0,), (0,)), ((), ())),
            preferred_element_type=jnp.float32,
        )
        by_layer = lax.psum_scatter(batch_grad * grad_scale, "cz", scatter_dimension=0, tiled=True)
        weight_grad = lax.psum_scatter(by_layer, "dp", scatter_dimension=0, tiled=True)
        attn_out = out_half.reshape(tok_rows, group * kv_width)[None]
        query_grad = query_part.reshape(tok_rows, group * kv_width)[None]
        key_grad = pair_half[:, :kv_width][None]
        value_grad = pair_half[:, kv_width:][None]
        return (attn_out, query_grad, key_grad, value_grad, weight_grad)

    return shards


def solution(mesh):
    n_data = mesh.shape["dp"]
    n_context = mesh.shape["ctx"]
    n_cw = 8 if n_context % 8 == 0 else n_context
    n_cz = n_context // n_cw
    split = Mesh(mesh.devices.reshape(n_data, n_cz, n_cw), ("dp", "cz", "cw"))
    tokens = P("dp", CTX, None)
    in_specs = (tokens, tokens, tokens, tokens, tokens, P("dp", None))
    out_specs = (tokens, tokens, tokens, tokens, P(("dp", "cz", "cw"), None))
    return jax.shard_map(
        make_shards(n_data, n_cz, n_cw),
        mesh=split,
        in_specs=in_specs,
        out_specs=out_specs,
        check_vma=False,
    )
```

```python
import math

import jax
import jax.numpy as jnp
from jax import lax
from jax.sharding import Mesh
from jax.sharding import PartitionSpec as P

D = 5120
HD = 128


NEGATIVE = -1e30
CTX = ("cz", "cw")


def shifted(block, distance, n_ctx):
    route = [(i - distance, i) for i in range(n_ctx) if 0 <= i - distance < n_ctx]
    return lax.ppermute(block, CTX, route)


def doc_index(lengths_row, positions):
    bounds = jnp.cumsum(lengths_row)
    return jnp.sum((positions[:, None] >= bounds[None, :]).astype(jnp.int32), axis=1)


def make_shards(n_data, n_cz, n_cw):
    n_context = n_cz * n_cw

    def shards(queries, keys, values, out_grad, layer_input, doc_lens):
        tok_rows = queries.shape[1]
        kv_width = keys.shape[2]
        heads_kv = kv_width // HD
        group = queries.shape[2] // kv_width
        inverse = 1.0 / math.sqrt(HD)
        blocks_back = min(8, n_context // 4)

        owned = D // (n_data * n_context)
        member = lax.axis_index("cw")
        chunks = layer_input[0].reshape(tok_rows, n_data, n_cz, n_cw, owned)
        chunks = chunks.transpose(3, 0, 2, 1, 4).reshape(n_cw, tok_rows, n_cz * n_data * owned)
        received = [lax.dynamic_index_in_dim(chunks, member, 0, keepdims=False)]
        for k in range(1, n_cw):
            route = [(i, (i + k) % n_cw) for i in range(n_cw)]
            outgoing = lax.dynamic_index_in_dim(chunks, (member + k) % n_cw, 0, keepdims=False)
            received.append(lax.ppermute(outgoing, "cw", route))
        column_share = jnp.concatenate(received[::-1], axis=0)

        own_pair = jnp.concatenate([keys[0], values[0]], axis=1)
        earlier = [shifted(own_pair, d, n_context) for d in range(blocks_back, 0, -1)]
        window_pair = jnp.concatenate(earlier + [own_pair], axis=0)
        span = window_pair.shape[0]
        key_win = window_pair[:, :kv_width].reshape(span, heads_kv, HD)
        value_win = window_pair[:, kv_width:].reshape(span, heads_kv, HD)
        device = lax.axis_index("cz") * n_cw + lax.axis_index("cw")
        query_pos = device * tok_rows + jnp.arange(tok_rows, dtype=jnp.int32)
        key_pos = (device - blocks_back) * tok_rows + jnp.arange(span, dtype=jnp.int32)
        query_ids = doc_index(doc_lens[0], query_pos)
        key_ids = doc_index(doc_lens[0], key_pos)
        allowed = (
            (key_pos[None, :] <= query_pos[:, None])
            & (key_ids[None, :] == query_ids[:, None])
            & (key_pos[None, :] >= 0)
        )
        query_blk = queries[0].reshape(tok_rows, heads_kv, group, HD)
        grad_blk = out_grad[0].reshape(tok_rows, heads_kv, group, HD)
        scores = (
            jnp.einsum("ighd,jgd->ghij", query_blk, key_win, preferred_element_type=jnp.float32)
            * inverse
        )
        scores = jnp.where(allowed[None, None], scores, NEGATIVE)
        peak = jnp.max(scores, axis=-1, keepdims=True)
        exponent = jnp.exp(scores - peak)
        probs = exponent / jnp.sum(exponent, axis=-1, keepdims=True)
        probs_half = probs.astype(jnp.bfloat16)
        output = jnp.einsum("ghij,jgd->ighd", probs_half, value_win, preferred_element_type=jnp.float32)
        out_half = output.astype(jnp.bfloat16)
        delta = jnp.einsum("ighd,ighd->ghi", grad_blk, out_half, preferred_element_type=jnp.float32)
        prob_grad = jnp.einsum(
            "ighd,jgd->ghij", grad_blk, value_win, preferred_element_type=jnp.float32
        )
        score_grad = (probs * (prob_grad - delta[..., None])).astype(jnp.bfloat16)
        query_part = (
            jnp.einsum("ghij,jgd->ighd", score_grad, key_win, preferred_element_type=jnp.float32)
            * inverse
        ).astype(jnp.bfloat16)
        key_part = (
            jnp.einsum("ghij,ighd->jgd", score_grad, query_blk, preferred_element_type=jnp.float32)
            * inverse
        )
        value_part = jnp.einsum(
            "ghij,ighd->jgd", probs_half, grad_blk, preferred_element_type=jnp.float32
        )
        pair_grad = jnp.concatenate(
            [key_part.reshape(span, kv_width), value_part.reshape(span, kv_width)], axis=1
        )

        column_share, pair_grad = lax.optimization_barrier((column_share, pair_grad))

        def block_back(distance):
            first_row = (blocks_back - distance) * tok_rows
            return pair_grad[first_row : first_row + tok_rows]

        total = block_back(0)
        for distance in range(1, blocks_back + 1):
            total = total + shifted(block_back(distance), -distance, n_context)
        pair_half = total.astype(jnp.bfloat16)

        grad_scale = 1.0 / math.sqrt(tok_rows * n_context * n_data)
        gathered = [pair_half]
        for k in range(1, n_cw):
            route = [(i, (i + k) % n_cw) for i in range(n_cw)]
            gathered.append(lax.ppermute(pair_half, "cw", route))
        group_grad = jnp.concatenate(gathered[::-1], axis=0)
        batch_grad = lax.dot_general(
            column_share,
            group_grad,
            (((0,), (0,)), ((), ())),
            preferred_element_type=jnp.float32,
        )
        by_layer = lax.psum_scatter(batch_grad * grad_scale, "cz", scatter_dimension=0, tiled=True)
        weight_grad = lax.psum_scatter(by_layer, "dp", scatter_dimension=0, tiled=True)
        attn_out = out_half.reshape(tok_rows, group * kv_width)[None]
        query_grad = query_part.reshape(tok_rows, group * kv_width)[None]
        key_grad = pair_half[:, :kv_width][None]
        value_grad = pair_half[:, kv_width:][None]
        return (attn_out, query_grad, key_grad, value_grad, weight_grad)

    return shards


def solution(mesh):
    n_data = mesh.shape["dp"]
    n_context = mesh.shape["ctx"]
    n_cw = 8 if n_context % 8 == 0 else n_context
    n_cz = n_context // n_cw
    split = Mesh(mesh.devices.reshape(n_data, n_cz, n_cw), ("dp", "cz", "cw"))
    tokens = P("dp", CTX, None)
    in_specs = (tokens, tokens, tokens, tokens, tokens, P("dp", None))
    out_specs = (tokens, tokens, tokens, tokens, P(("dp", "cz", "cw"), None))
    return jax.shard_map(
        make_shards(n_data, n_cz, n_cw),
        mesh=split,
        in_specs=in_specs,
        out_specs=out_specs,
        check_vma=False,
    )
```

```python
import functools
import math

import jax
import jax.numpy as jnp
from jax import lax
from jax.experimental import pallas as pl
from jax.sharding import Mesh
from jax.sharding import PartitionSpec as P

D = 5120
HD = 128


NEGATIVE = -1e30
CTX = ("cz", "cw")


def shifted(block, distance, n_ctx):
    route = [(i - distance, i) for i in range(n_ctx) if 0 <= i - distance < n_ctx]
    return lax.ppermute(block, CTX, route)


def doc_index(lengths_row, positions):
    bounds = jnp.cumsum(lengths_row)
    return jnp.sum((positions[:, None] >= bounds[None, :]).astype(jnp.int32), axis=1)


def attn_kernel(qid_ref, kid_ref, q_ref, do_ref, k_ref, v_ref, o_ref, dq_ref, dk_ref, dv_ref, *, group, inverse):
    k = k_ref[...]
    v = v_ref[...]
    rows = q_ref.shape[0]
    span = k.shape[0]
    row = lax.broadcasted_iota(jnp.int32, (rows, span), 0)
    col = lax.broadcasted_iota(jnp.int32, (rows, span), 1)
    allowed = (col <= row + (span - rows)) & (kid_ref[...] == qid_ref[...])
    dk = jnp.zeros((span, HD), jnp.float32)
    dv = jnp.zeros((span, HD), jnp.float32)
    for h in range(group):
        cols = slice(h * HD, (h + 1) * HD)
        q = q_ref[:, cols]
        do = do_ref[:, cols]
        s = lax.dot_general(q, k, (((1,), (1,)), ((), ())), preferred_element_type=jnp.float32) * inverse
        s = jnp.where(allowed, s, NEGATIVE)
        e = jnp.exp(s - jnp.max(s, axis=1, keepdims=True))
        p = e / jnp.sum(e, axis=1, keepdims=True)
        ph = p.astype(jnp.bfloat16)
        oh = jnp.dot(ph, v, preferred_element_type=jnp.float32).astype(jnp.bfloat16)
        o_ref[:, cols] = oh
        delta = jnp.sum(do.astype(jnp.float32) * oh.astype(jnp.float32), axis=1, keepdims=True)
        dp = lax.dot_general(do, v, (((1,), (1,)), ((), ())), preferred_element_type=jnp.float32)
        ds = (p * (dp - delta)).astype(jnp.bfloat16)
        dq_ref[:, cols] = (jnp.dot(ds, k, preferred_element_type=jnp.float32) * inverse).astype(jnp.bfloat16)
        dk = dk + lax.dot_general(ds, q, (((0,), (0,)), ((), ())), preferred_element_type=jnp.float32)
        dv = dv + lax.dot_general(ph, do, (((0,), (0,)), ((), ())), preferred_element_type=jnp.float32)
    dk_ref[...] = dk * inverse
    dv_ref[...] = dv


def attention(query_ids, key_ids, queries, out_grad, window_pair, heads_kv):
    rows, width = queries.shape
    span = window_pair.shape[0]
    group = width // (heads_kv * HD)
    kernel = functools.partial(attn_kernel, group=group, inverse=1.0 / math.sqrt(HD))
    wide = group * HD
    return pl.pallas_call(
        kernel,
        grid=(heads_kv,),
        in_specs=[
            pl.BlockSpec((rows, 1), lambda g: (0, 0)),
            pl.BlockSpec((1, span), lambda g: (0, 0)),
            pl.BlockSpec((rows, wide), lambda g: (0, g)),
            pl.BlockSpec((rows, wide), lambda g: (0, g)),
            pl.BlockSpec((span, HD), lambda g: (0, g)),
            pl.BlockSpec((span, HD), lambda g: (0, heads_kv + g)),
        ],
        out_specs=[
            pl.BlockSpec((rows, wide), lambda g: (0, g)),
            pl.BlockSpec((rows, wide), lambda g: (0, g)),
            pl.BlockSpec((span, HD), lambda g: (0, g)),
            pl.BlockSpec((span, HD), lambda g: (0, g)),
        ],
        out_shape=[
            jax.ShapeDtypeStruct((rows, width), jnp.bfloat16),
            jax.ShapeDtypeStruct((rows, width), jnp.bfloat16),
            jax.ShapeDtypeStruct((span, heads_kv * HD), jnp.float32),
            jax.ShapeDtypeStruct((span, heads_kv * HD), jnp.float32),
        ],
    )(query_ids.reshape(rows, 1), key_ids.reshape(1, span), queries, out_grad, window_pair, window_pair)


def make_shards(n_data, n_cz, n_cw):
    n_context = n_cz * n_cw

    def shards(queries, keys, values, out_grad, layer_input, doc_lens):
        tok_rows = queries.shape[1]
        kv_width = keys.shape[2]
        heads_kv = kv_width // HD
        group = queries.shape[2] // kv_width
        inverse = 1.0 / math.sqrt(HD)
        blocks_back = min(8, n_context // 4)

        owned = D // (n_data * n_context)
        member = lax.axis_index("cw")
        chunks = layer_input[0].reshape(tok_rows, n_data, n_cz, n_cw, owned)
        chunks = chunks.transpose(3, 0, 2, 1, 4).reshape(n_cw, tok_rows, n_cz * n_data * owned)
        received = [lax.dynamic_index_in_dim(chunks, member, 0, keepdims=False)]
        for k in range(1, n_cw):
            route = [(i, (i + k) % n_cw) for i in range(n_cw)]
            outgoing = lax.dynamic_index_in_dim(chunks, (member + k) % n_cw, 0, keepdims=False)
            received.append(lax.ppermute(outgoing, "cw", route))
        column_share = jnp.concatenate(received[::-1], axis=0)

        own_pair = jnp.concatenate([keys[0], values[0]], axis=1)
        earlier = [shifted(own_pair, d, n_context) for d in range(blocks_back, 0, -1)]
        window_pair = jnp.concatenate(earlier + [own_pair], axis=0)
        span = window_pair.shape[0]
        device = lax.axis_index("cz") * n_cw + lax.axis_index("cw")
        query_pos = device * tok_rows + jnp.arange(tok_rows, dtype=jnp.int32)
        key_pos = (device - blocks_back) * tok_rows + jnp.arange(span, dtype=jnp.int32)
        query_ids = doc_index(doc_lens[0], query_pos)
        key_ids = jnp.where(key_pos >= 0, doc_index(doc_lens[0], key_pos), -1)
        out_half, query_part, key_part, value_part = attention(
            query_ids, key_ids, queries[0], out_grad[0], window_pair, heads_kv
        )
        pair_grad = jnp.concatenate([key_part, value_part], axis=1)

        column_share, pair_grad = lax.optimization_barrier((column_share, pair_grad))

        def block_back(distance):
            first_row = (blocks_back - distance) * tok_rows
            return pair_grad[first_row : first_row + tok_rows]

        total = block_back(0)
        for distance in range(1, blocks_back + 1):
            total = total + shifted(block_back(distance), -distance, n_context)
        pair_half = total.astype(jnp.bfloat16)

        grad_scale = 1.0 / math.sqrt(tok_rows * n_context * n_data)
        gathered = [pair_half]
        for k in range(1, n_cw):
            route = [(i, (i + k) % n_cw) for i in range(n_cw)]
            gathered.append(lax.ppermute(pair_half, "cw", route))
        group_grad = jnp.concatenate(gathered[::-1], axis=0)
        batch_grad = lax.dot_general(
            column_share,
            group_grad,
            (((0,), (0,)), ((), ())),
            preferred_element_type=jnp.float32,
        )
        by_layer = lax.psum_scatter(batch_grad * grad_scale, "cz", scatter_dimension=0, tiled=True)
        weight_grad = lax.psum_scatter(by_layer, "dp", scatter_dimension=0, tiled=True)
        attn_out = out_half[None]
        query_grad = query_part[None]
        key_grad = pair_half[:, :kv_width][None]
        value_grad = pair_half[:, kv_width:][None]
        return (attn_out, query_grad, key_grad, value_grad, weight_grad)

    return shards


def solution(mesh):
    n_data = mesh.shape["dp"]
    n_context = mesh.shape["ctx"]
    n_cw = 8 if n_context % 8 == 0 else n_context
    n_cz = n_context // n_cw
    split = Mesh(mesh.devices.reshape(n_data, n_cz, n_cw), ("dp", "cz", "cw"))
    tokens = P("dp", CTX, None)
    in_specs = (tokens, tokens, tokens, tokens, tokens, P("dp", None))
    out_specs = (tokens, tokens, tokens, tokens, P(("dp", "cz", "cw"), None))
    return jax.shard_map(
        make_shards(n_data, n_cz, n_cw),
        mesh=split,
        in_specs=in_specs,
        out_specs=out_specs,
        check_vma=False,
    )
```

```python
import functools
import math

import jax
import jax.numpy as jnp
from jax import lax
from jax.experimental import pallas as pl
from jax.sharding import Mesh
from jax.sharding import PartitionSpec as P

D = 5120
HD = 128


NEGATIVE = -1e30
CTX = ("cz", "cw")


def shifted(block, distance, n_ctx):
    route = [(i - distance, i) for i in range(n_ctx) if 0 <= i - distance < n_ctx]
    return lax.ppermute(block, CTX, route)


def doc_index(lengths_row, positions):
    bounds = jnp.cumsum(lengths_row)
    return jnp.sum((positions[:, None] >= bounds[None, :]).astype(jnp.int32), axis=1)


def attn_kernel(qid_ref, kid_ref, q_ref, do_ref, k_ref, v_ref, o_ref, dq_ref, dk_ref, dv_ref, *, group, inverse):
    k = k_ref[...]
    v = v_ref[...]
    rows = q_ref.shape[0]
    span = k.shape[0]
    row = lax.broadcasted_iota(jnp.int32, (rows, span), 0)
    col = lax.broadcasted_iota(jnp.int32, (rows, span), 1)
    allowed = (col <= row + (span - rows)) & (kid_ref[...] == qid_ref[...])
    dk = jnp.zeros((span, HD), jnp.float32)
    dv = jnp.zeros((span, HD), jnp.float32)
    for h in range(group):
        cols = slice(h * HD, (h + 1) * HD)
        q = q_ref[:, cols]
        do = do_ref[:, cols]
        s = lax.dot_general(q, k, (((1,), (1,)), ((), ())), preferred_element_type=jnp.float32) * inverse
        s = jnp.where(allowed, s, NEGATIVE)
        e = jnp.exp(s - jnp.max(s, axis=1, keepdims=True))
        p = e / jnp.sum(e, axis=1, keepdims=True)
        ph = p.astype(jnp.bfloat16)
        oh = jnp.dot(ph, v, preferred_element_type=jnp.float32).astype(jnp.bfloat16)
        o_ref[:, cols] = oh
        delta = jnp.sum(do.astype(jnp.float32) * oh.astype(jnp.float32), axis=1, keepdims=True)
        dp = lax.dot_general(do, v, (((1,), (1,)), ((), ())), preferred_element_type=jnp.float32)
        ds = (p * (dp - delta)).astype(jnp.bfloat16)
        dq_ref[:, cols] = (jnp.dot(ds, k, preferred_element_type=jnp.float32) * inverse).astype(jnp.bfloat16)
        dk = dk + lax.dot_general(ds, q, (((0,), (0,)), ((), ())), preferred_element_type=jnp.float32)
        dv = dv + lax.dot_general(ph, do, (((0,), (0,)), ((), ())), preferred_element_type=jnp.float32)
    dk_ref[...] = dk * inverse
    dv_ref[...] = dv


def attention(query_ids, key_ids, queries, out_grad, window_pair, heads_kv):
    rows, width = queries.shape
    span = window_pair.shape[0]
    group = width // (heads_kv * HD)
    kernel = functools.partial(attn_kernel, group=group, inverse=1.0 / math.sqrt(HD))
    wide = group * HD
    return pl.pallas_call(
        kernel,
        grid=(heads_kv,),
        in_specs=[
            pl.BlockSpec((rows, 1), lambda g: (0, 0)),
            pl.BlockSpec((1, span), lambda g: (0, 0)),
            pl.BlockSpec((rows, wide), lambda g: (0, g)),
            pl.BlockSpec((rows, wide), lambda g: (0, g)),
            pl.BlockSpec((span, HD), lambda g: (0, g)),
            pl.BlockSpec((span, HD), lambda g: (0, heads_kv + g)),
        ],
        out_specs=[
            pl.BlockSpec((rows, wide), lambda g: (0, g)),
            pl.BlockSpec((rows, wide), lambda g: (0, g)),
            pl.BlockSpec((span, HD), lambda g: (0, g)),
            pl.BlockSpec((span, HD), lambda g: (0, g)),
        ],
        out_shape=[
            jax.ShapeDtypeStruct((rows, width), jnp.bfloat16),
            jax.ShapeDtypeStruct((rows, width), jnp.bfloat16),
            jax.ShapeDtypeStruct((span, heads_kv * HD), jnp.float32),
            jax.ShapeDtypeStruct((span, heads_kv * HD), jnp.float32),
        ],
    )(query_ids.reshape(rows, 1), key_ids.reshape(1, span), queries, out_grad, window_pair, window_pair)


def make_shards(n_data, n_cz, n_cw):
    n_context = n_cz * n_cw

    def shards(queries, keys, values, out_grad, layer_input, doc_lens):
        tok_rows = queries.shape[1]
        kv_width = keys.shape[2]
        heads_kv = kv_width // HD
        group = queries.shape[2] // kv_width
        inverse = 1.0 / math.sqrt(HD)
        blocks_back = min(8, n_context // 4)

        owned = D // (n_data * n_context)

        own_pair = jnp.concatenate([keys[0], values[0]], axis=1)
        earlier = [shifted(own_pair, d, n_context) for d in range(blocks_back, 0, -1)]
        window_pair = jnp.concatenate(earlier + [own_pair], axis=0)
        member = lax.axis_index("cw")
        chunks = layer_input[0].reshape(tok_rows, n_data, n_cz, n_cw, owned)
        chunks, window_pair = lax.optimization_barrier((chunks, window_pair))
        chunks = chunks.transpose(3, 0, 2, 1, 4).reshape(n_cw, tok_rows, n_cz * n_data * owned)
        received = [lax.dynamic_index_in_dim(chunks, member, 0, keepdims=False)]
        for k in range(1, n_cw):
            route = [(i, (i + k) % n_cw) for i in range(n_cw)]
            outgoing = lax.dynamic_index_in_dim(chunks, (member + k) % n_cw, 0, keepdims=False)
            received.append(lax.ppermute(outgoing, "cw", route))
        column_share = jnp.concatenate(received[::-1], axis=0)
        span = window_pair.shape[0]
        device = lax.axis_index("cz") * n_cw + lax.axis_index("cw")
        query_pos = device * tok_rows + jnp.arange(tok_rows, dtype=jnp.int32)
        key_pos = (device - blocks_back) * tok_rows + jnp.arange(span, dtype=jnp.int32)
        query_ids = doc_index(doc_lens[0], query_pos)
        key_ids = jnp.where(key_pos >= 0, doc_index(doc_lens[0], key_pos), -1)
        out_half, query_part, key_part, value_part = attention(
            query_ids, key_ids, queries[0], out_grad[0], window_pair, heads_kv
        )
        column_share, key_part, value_part = lax.optimization_barrier(
            (column_share, key_part, value_part)
        )
        grad_scale = 1.0 / math.sqrt(tok_rows * n_context * n_data)

        def finish(part_grad):
            def block_back(distance):
                first_row = (blocks_back - distance) * tok_rows
                return part_grad[first_row : first_row + tok_rows]

            total = block_back(0)
            for distance in range(1, blocks_back + 1):
                total = total + shifted(block_back(distance), -distance, n_context)
            half = total.astype(jnp.bfloat16)
            gathered = [half]
            for k in range(1, n_cw):
                route = [(i, (i + k) % n_cw) for i in range(n_cw)]
                gathered.append(lax.ppermute(half, "cw", route))
            group_grad = jnp.concatenate(gathered[::-1], axis=0)
            batch_grad = lax.dot_general(
                column_share,
                group_grad,
                (((0,), (0,)), ((), ())),
                preferred_element_type=jnp.float32,
            )
            by_layer = lax.psum_scatter(batch_grad * grad_scale, "cz", scatter_dimension=0, tiled=True)
            return half, lax.psum_scatter(by_layer, "dp", scatter_dimension=0, tiled=True)

        key_half, key_weight = finish(key_part)
        value_half, value_weight = finish(value_part)
        weight_grad = jnp.concatenate([key_weight, value_weight], axis=1)
        attn_out = out_half[None]
        query_grad = query_part[None]
        key_grad = key_half[None]
        value_grad = value_half[None]
        return (attn_out, query_grad, key_grad, value_grad, weight_grad)

    return shards


def solution(mesh):
    n_data = mesh.shape["dp"]
    n_context = mesh.shape["ctx"]
    n_cw = 8 if n_context % 8 == 0 else n_context
    n_cz = n_context // n_cw
    split = Mesh(mesh.devices.reshape(n_data, n_cz, n_cw), ("dp", "cz", "cw"))
    tokens = P("dp", CTX, None)
    in_specs = (tokens, tokens, tokens, tokens, tokens, P("dp", None))
    out_specs = (tokens, tokens, tokens, tokens, P(("dp", "cz", "cw"), None))
    return jax.shard_map(
        make_shards(n_data, n_cz, n_cw),
        mesh=split,
        in_specs=in_specs,
        out_specs=out_specs,
        check_vma=False,
    )
```

```python
import functools
import math

import jax
import jax.numpy as jnp
from jax import lax
from jax.experimental import pallas as pl
from jax.sharding import Mesh
from jax.sharding import PartitionSpec as P

D = 5120
HD = 128


NEGATIVE = -1e30
CTX = ("cz", "cw")


def shifted(block, distance, n_ctx):
    route = [(i - distance, i) for i in range(n_ctx) if 0 <= i - distance < n_ctx]
    return lax.ppermute(block, CTX, route)


def doc_index(lengths_row, positions):
    bounds = jnp.cumsum(lengths_row)
    return jnp.sum((positions[:, None] >= bounds[None, :]).astype(jnp.int32), axis=1)


def attn_kernel(qid_ref, kid_ref, q_ref, do_ref, k_ref, v_ref, o_ref, dq_ref, dk_ref, dv_ref, *, group, inverse):
    k = k_ref[...]
    v = v_ref[...]
    rows = q_ref.shape[0]
    span = k.shape[0]
    row = lax.broadcasted_iota(jnp.int32, (rows, span), 0)
    col = lax.broadcasted_iota(jnp.int32, (rows, span), 1)
    allowed = (col <= row + (span - rows)) & (kid_ref[...] == qid_ref[...])
    dk = jnp.zeros((span, HD), jnp.float32)
    dv = jnp.zeros((span, HD), jnp.float32)
    for h in range(group):
        cols = slice(h * HD, (h + 1) * HD)
        q = q_ref[:, cols]
        do = do_ref[:, cols]
        s = lax.dot_general(q, k, (((1,), (1,)), ((), ())), preferred_element_type=jnp.float32) * inverse
        s = jnp.where(allowed, s, NEGATIVE)
        e = jnp.exp(s - jnp.max(s, axis=1, keepdims=True))
        p = e / jnp.sum(e, axis=1, keepdims=True)
        ph = p.astype(jnp.bfloat16)
        oh = jnp.dot(ph, v, preferred_element_type=jnp.float32).astype(jnp.bfloat16)
        o_ref[:, cols] = oh
        delta = jnp.sum(do.astype(jnp.float32) * oh.astype(jnp.float32), axis=1, keepdims=True)
        dp = lax.dot_general(do, v, (((1,), (1,)), ((), ())), preferred_element_type=jnp.float32)
        ds = (p * (dp - delta)).astype(jnp.bfloat16)
        dq_ref[:, cols] = (jnp.dot(ds, k, preferred_element_type=jnp.float32) * inverse).astype(jnp.bfloat16)
        dk = dk + lax.dot_general(ds, q, (((0,), (0,)), ((), ())), preferred_element_type=jnp.float32)
        dv = dv + lax.dot_general(ph, do, (((0,), (0,)), ((), ())), preferred_element_type=jnp.float32)
    dk_ref[...] = dk * inverse
    dv_ref[...] = dv


def attention(query_ids, key_ids, queries, out_grad, window_pair, heads_kv):
    rows, width = queries.shape
    span = window_pair.shape[0]
    group = width // (heads_kv * HD)
    kernel = functools.partial(attn_kernel, group=group, inverse=1.0 / math.sqrt(HD))
    wide = group * HD
    return pl.pallas_call(
        kernel,
        grid=(heads_kv,),
        in_specs=[
            pl.BlockSpec((rows, 1), lambda g: (0, 0)),
            pl.BlockSpec((1, span), lambda g: (0, 0)),
            pl.BlockSpec((rows, wide), lambda g: (0, g)),
            pl.BlockSpec((rows, wide), lambda g: (0, g)),
            pl.BlockSpec((span, HD), lambda g: (0, g)),
            pl.BlockSpec((span, HD), lambda g: (0, heads_kv + g)),
        ],
        out_specs=[
            pl.BlockSpec((rows, wide), lambda g: (0, g)),
            pl.BlockSpec((rows, wide), lambda g: (0, g)),
            pl.BlockSpec((span, HD), lambda g: (0, g)),
            pl.BlockSpec((span, HD), lambda g: (0, g)),
        ],
        out_shape=[
            jax.ShapeDtypeStruct((rows, width), jnp.bfloat16),
            jax.ShapeDtypeStruct((rows, width), jnp.bfloat16),
            jax.ShapeDtypeStruct((span, heads_kv * HD), jnp.float32),
            jax.ShapeDtypeStruct((span, heads_kv * HD), jnp.float32),
        ],
    )(query_ids.reshape(rows, 1), key_ids.reshape(1, span), queries, out_grad, window_pair, window_pair)


def make_shards(n_data, n_cz, n_cw):
    n_context = n_cz * n_cw

    def shards(queries, keys, values, out_grad, layer_input, doc_lens):
        tok_rows = queries.shape[1]
        kv_width = keys.shape[2]
        heads_kv = kv_width // HD
        group = queries.shape[2] // kv_width
        inverse = 1.0 / math.sqrt(HD)
        blocks_back = min(8, n_context // 4)

        owned = D // (n_data * n_context)

        own_pair = jnp.concatenate([keys[0], values[0]], axis=1)
        earlier = [shifted(own_pair, d, n_context) for d in range(blocks_back, 0, -1)]
        window_pair = jnp.concatenate(earlier + [own_pair], axis=0)
        member = lax.axis_index("cw")
        chunks = layer_input[0].reshape(tok_rows, n_data, n_cz, n_cw, owned)
        chunks, window_pair = lax.optimization_barrier((chunks, window_pair))
        chunks = chunks.transpose(3, 0, 2, 1, 4).reshape(n_cw, tok_rows, n_cz * n_data * owned)
        received = [lax.dynamic_index_in_dim(chunks, member, 0, keepdims=False)]
        for k in range(1, n_cw):
            route = [(i, (i + k) % n_cw) for i in range(n_cw)]
            outgoing = lax.dynamic_index_in_dim(chunks, (member + k) % n_cw, 0, keepdims=False)
            received.append(lax.ppermute(outgoing, "cw", route))
        column_share = jnp.concatenate(received[::-1], axis=0)
        span = window_pair.shape[0]
        device = lax.axis_index("cz") * n_cw + lax.axis_index("cw")
        query_pos = device * tok_rows + jnp.arange(tok_rows, dtype=jnp.int32)
        key_pos = (device - blocks_back) * tok_rows + jnp.arange(span, dtype=jnp.int32)
        query_ids = doc_index(doc_lens[0], query_pos)
        key_ids = jnp.where(key_pos >= 0, doc_index(doc_lens[0], key_pos), -1)
        out_half, query_part, key_part, value_part = attention(
            query_ids, key_ids, queries[0], out_grad[0], window_pair, heads_kv
        )
        column_share, key_part, value_part = lax.optimization_barrier(
            (column_share, key_part, value_part)
        )
        grad_scale = 1.0 / math.sqrt(tok_rows * n_context * n_data)

        pair_grad = jnp.concatenate([key_part, value_part], axis=1)

        def block_back(distance):
            first_row = (blocks_back - distance) * tok_rows
            return pair_grad[first_row : first_row + tok_rows]

        total = block_back(0)
        for distance in range(1, blocks_back + 1):
            sent = block_back(distance).astype(jnp.bfloat16)
            total = total + shifted(sent, -distance, n_context).astype(jnp.float32)
        pair_half = total.astype(jnp.bfloat16)
        gathered = [pair_half]
        for k in range(1, n_cw):
            route = [(i, (i + k) % n_cw) for i in range(n_cw)]
            gathered.append(lax.ppermute(pair_half, "cw", route))
        group_grad = jnp.concatenate(gathered[::-1], axis=0)
        batch_grad = lax.dot_general(
            column_share,
            group_grad,
            (((0,), (0,)), ((), ())),
            preferred_element_type=jnp.float32,
        )
        by_layer = lax.psum_scatter(batch_grad * grad_scale, "cz", scatter_dimension=0, tiled=True)
        weight_grad = lax.psum_scatter(by_layer, "dp", scatter_dimension=0, tiled=True)
        attn_out = out_half[None]
        query_grad = query_part[None]
        key_grad = pair_half[:, :kv_width][None]
        value_grad = pair_half[:, kv_width:][None]
        return (attn_out, query_grad, key_grad, value_grad, weight_grad)

    return shards


def solution(mesh):
    n_data = mesh.shape["dp"]
    n_context = mesh.shape["ctx"]
    n_cw = 8 if n_context % 8 == 0 else n_context
    n_cz = n_context // n_cw
    split = Mesh(mesh.devices.reshape(n_data, n_cz, n_cw), ("dp", "cz", "cw"))
    tokens = P("dp", CTX, None)
    in_specs = (tokens, tokens, tokens, tokens, tokens, P("dp", None))
    out_specs = (tokens, tokens, tokens, tokens, P(("dp", "cz", "cw"), None))
    return jax.shard_map(
        make_shards(n_data, n_cz, n_cw),
        mesh=split,
        in_specs=in_specs,
        out_specs=out_specs,
        check_vma=False,
    )
```

```python
import functools
import math

import jax
import jax.numpy as jnp
from jax import lax
from jax.experimental import pallas as pl
from jax.sharding import Mesh
from jax.sharding import PartitionSpec as P

D = 5120
HD = 128


NEGATIVE = -1e30
CTX = ("cz", "cw")


def shifted(block, distance, n_ctx):
    route = [(i - distance, i) for i in range(n_ctx) if 0 <= i - distance < n_ctx]
    return lax.ppermute(block, CTX, route)


def doc_index(lengths_row, positions):
    bounds = jnp.cumsum(lengths_row)
    return jnp.sum((positions[:, None] >= bounds[None, :]).astype(jnp.int32), axis=1)


def attn_kernel(qid_ref, kid_ref, q_ref, do_ref, k_ref, v_ref, o_ref, dq_ref, dk_ref, dv_ref, *, group, inverse):
    k = k_ref[...]
    v = v_ref[...]
    rows = q_ref.shape[0]
    span = k.shape[0]
    row = lax.broadcasted_iota(jnp.int32, (rows, span), 0)
    col = lax.broadcasted_iota(jnp.int32, (rows, span), 1)
    allowed = (col <= row + (span - rows)) & (kid_ref[...] == qid_ref[...])
    dk = jnp.zeros((span, HD), jnp.float32)
    dv = jnp.zeros((span, HD), jnp.float32)
    for h in range(group):
        cols = slice(h * HD, (h + 1) * HD)
        q = q_ref[:, cols]
        do = do_ref[:, cols]
        s = lax.dot_general(q, k, (((1,), (1,)), ((), ())), preferred_element_type=jnp.float32) * inverse
        s = jnp.where(allowed, s, NEGATIVE)
        e = jnp.exp(s - jnp.max(s, axis=1, keepdims=True))
        p = e / jnp.sum(e, axis=1, keepdims=True)
        ph = p.astype(jnp.bfloat16)
        oh = jnp.dot(ph, v, preferred_element_type=jnp.float32).astype(jnp.bfloat16)
        o_ref[:, cols] = oh
        delta = jnp.sum(do.astype(jnp.float32) * oh.astype(jnp.float32), axis=1, keepdims=True)
        dp = lax.dot_general(do, v, (((1,), (1,)), ((), ())), preferred_element_type=jnp.float32)
        ds = (p * (dp - delta)).astype(jnp.bfloat16)
        dq_ref[:, cols] = (jnp.dot(ds, k, preferred_element_type=jnp.float32) * inverse).astype(jnp.bfloat16)
        dk = dk + lax.dot_general(ds, q, (((0,), (0,)), ((), ())), preferred_element_type=jnp.float32)
        dv = dv + lax.dot_general(ph, do, (((0,), (0,)), ((), ())), preferred_element_type=jnp.float32)
    dk_ref[...] = dk * inverse
    dv_ref[...] = dv


def attention(query_ids, key_ids, queries, out_grad, window_pair, heads_kv):
    rows, width = queries.shape
    span = window_pair.shape[0]
    group = width // (heads_kv * HD)
    kernel = functools.partial(attn_kernel, group=group, inverse=1.0 / math.sqrt(HD))
    wide = group * HD
    return pl.pallas_call(
        kernel,
        grid=(heads_kv,),
        in_specs=[
            pl.BlockSpec((rows, 1), lambda g: (0, 0)),
            pl.BlockSpec((1, span), lambda g: (0, 0)),
            pl.BlockSpec((rows, wide), lambda g: (0, g)),
            pl.BlockSpec((rows, wide), lambda g: (0, g)),
            pl.BlockSpec((span, HD), lambda g: (0, g)),
            pl.BlockSpec((span, HD), lambda g: (0, heads_kv + g)),
        ],
        out_specs=[
            pl.BlockSpec((rows, wide), lambda g: (0, g)),
            pl.BlockSpec((rows, wide), lambda g: (0, g)),
            pl.BlockSpec((span, HD), lambda g: (0, g)),
            pl.BlockSpec((span, HD), lambda g: (0, g)),
        ],
        out_shape=[
            jax.ShapeDtypeStruct((rows, width), jnp.bfloat16),
            jax.ShapeDtypeStruct((rows, width), jnp.bfloat16),
            jax.ShapeDtypeStruct((span, heads_kv * HD), jnp.float32),
            jax.ShapeDtypeStruct((span, heads_kv * HD), jnp.float32),
        ],
    )(query_ids.reshape(rows, 1), key_ids.reshape(1, span), queries, out_grad, window_pair, window_pair)


def make_shards(n_data, n_cz, n_cw):
    n_context = n_cz * n_cw

    def shards(queries, keys, values, out_grad, layer_input, doc_lens):
        tok_rows = queries.shape[1]
        kv_width = keys.shape[2]
        heads_kv = kv_width // HD
        group = queries.shape[2] // kv_width
        inverse = 1.0 / math.sqrt(HD)
        blocks_back = min(8, n_context // 4)

        owned = D // (n_data * n_context)

        own_pair = jnp.concatenate([keys[0], values[0]], axis=1)
        earlier = [shifted(own_pair, d, n_context) for d in range(blocks_back, 0, -1)]
        window_pair = jnp.concatenate(earlier + [own_pair], axis=0)
        member = lax.axis_index("cw")
        chunks = layer_input[0].reshape(tok_rows, n_data, n_cz, n_cw, owned)
        chunks, window_pair = lax.optimization_barrier((chunks, window_pair))
        chunks = chunks.transpose(3, 0, 1, 2, 4).reshape(n_cw, tok_rows, n_data * n_cz * owned)
        received = [lax.dynamic_index_in_dim(chunks, member, 0, keepdims=False)]
        for k in range(1, n_cw):
            route = [(i, (i + k) % n_cw) for i in range(n_cw)]
            outgoing = lax.dynamic_index_in_dim(chunks, (member + k) % n_cw, 0, keepdims=False)
            received.append(lax.ppermute(outgoing, "cw", route))
        column_share = jnp.concatenate(received[::-1], axis=0)
        span = window_pair.shape[0]
        device = lax.axis_index("cz") * n_cw + lax.axis_index("cw")
        query_pos = device * tok_rows + jnp.arange(tok_rows, dtype=jnp.int32)
        key_pos = (device - blocks_back) * tok_rows + jnp.arange(span, dtype=jnp.int32)
        query_ids = doc_index(doc_lens[0], query_pos)
        key_ids = jnp.where(key_pos >= 0, doc_index(doc_lens[0], key_pos), -1)
        out_half, query_part, key_part, value_part = attention(
            query_ids, key_ids, queries[0], out_grad[0], window_pair, heads_kv
        )
        column_share, key_part, value_part = lax.optimization_barrier(
            (column_share, key_part, value_part)
        )
        grad_scale = 1.0 / math.sqrt(tok_rows * n_context * n_data)

        pair_grad = jnp.concatenate([key_part, value_part], axis=1)

        def block_back(distance):
            first_row = (blocks_back - distance) * tok_rows
            return pair_grad[first_row : first_row + tok_rows]

        total = block_back(0)
        for distance in range(1, blocks_back + 1):
            sent = block_back(distance).astype(jnp.bfloat16)
            total = total + shifted(sent, -distance, n_context).astype(jnp.float32)
        pair_half = total.astype(jnp.bfloat16)
        gathered = [pair_half]
        for k in range(1, n_cw):
            route = [(i, (i + k) % n_cw) for i in range(n_cw)]
            gathered.append(lax.ppermute(pair_half, "cw", route))
        group_grad = jnp.concatenate(gathered[::-1], axis=0)
        batch_grad = lax.dot_general(
            column_share,
            group_grad,
            (((0,), (0,)), ((), ())),
            preferred_element_type=jnp.float32,
        )
        owners = n_data * n_cz
        share = (batch_grad * grad_scale).reshape(owners, owned * 2 * kv_width // 128, 128)
        weight_grad = lax.psum_scatter(share, ("dp", "cz"), scatter_dimension=0, tiled=True)
        weight_grad = weight_grad.reshape(owned, 2 * kv_width)
        attn_out = out_half[None]
        query_grad = query_part[None]
        key_grad = pair_half[:, :kv_width][None]
        value_grad = pair_half[:, kv_width:][None]
        return (attn_out, query_grad, key_grad, value_grad, weight_grad)

    return shards


def solution(mesh):
    n_data = mesh.shape["dp"]
    n_context = mesh.shape["ctx"]
    n_cw = 8 if n_context % 8 == 0 else n_context
    n_cz = n_context // n_cw
    split = Mesh(mesh.devices.reshape(n_data, n_cz, n_cw), ("dp", "cz", "cw"))
    tokens = P("dp", CTX, None)
    in_specs = (tokens, tokens, tokens, tokens, tokens, P("dp", None))
    out_specs = (tokens, tokens, tokens, tokens, P(("dp", "cz", "cw"), None))
    return jax.shard_map(
        make_shards(n_data, n_cz, n_cw),
        mesh=split,
        in_specs=in_specs,
        out_specs=out_specs,
        check_vma=False,
    )
```

```python
import functools
import math

import jax
import jax.numpy as jnp
from jax import lax
from jax.experimental import pallas as pl
from jax.experimental.pallas import tpu as pltpu
from jax.sharding import Mesh
from jax.sharding import PartitionSpec as P

D = 5120
HD = 128


NEGATIVE = -1e30
CTX = ("cz", "cw")


def shifted(block, distance, n_ctx):
    route = [(i - distance, i) for i in range(n_ctx) if 0 <= i - distance < n_ctx]
    return lax.ppermute(block, CTX, route)


def doc_index(lengths_row, positions):
    bounds = jnp.cumsum(lengths_row)
    return jnp.sum((positions[:, None] >= bounds[None, :]).astype(jnp.int32), axis=1)


def attn_kernel(first_ref, qid_ref, kid_ref, q_ref, do_ref, k_ref, v_ref, o_ref, dq_ref, dk_ref, dv_ref, *, group, inverse, spans):
    rows = q_ref.shape[0]
    full = k_ref.shape[0]
    dk_ref[...] = jnp.zeros(dk_ref.shape, dk_ref.dtype)
    dv_ref[...] = jnp.zeros(dv_ref.shape, dv_ref.dtype)

    def run(span):
        skip = full - span
        k = k_ref[skip:, :]
        v = v_ref[skip:, :]
        row = lax.broadcasted_iota(jnp.int32, (rows, span), 0)
        col = lax.broadcasted_iota(jnp.int32, (rows, span), 1)
        allowed = (col <= row + (span - rows)) & (kid_ref[:, skip:] == qid_ref[...])
        def head(h, sums):
            dk, dv = sums
            cols = pl.ds(pl.multiple_of(h * HD, HD), HD)
            q = q_ref[:, cols]
            do = do_ref[:, cols]
            s = lax.dot_general(q, k, (((1,), (1,)), ((), ())), preferred_element_type=jnp.float32) * inverse
            s = jnp.where(allowed, s, NEGATIVE)
            e = jnp.exp(s - jnp.max(s, axis=1, keepdims=True))
            p = e / jnp.sum(e, axis=1, keepdims=True)
            ph = p.astype(jnp.bfloat16)
            oh = jnp.dot(ph, v, preferred_element_type=jnp.float32).astype(jnp.bfloat16)
            o_ref[:, cols] = oh
            delta = jnp.sum(do.astype(jnp.float32) * oh.astype(jnp.float32), axis=1, keepdims=True)
            dp = lax.dot_general(do, v, (((1,), (1,)), ((), ())), preferred_element_type=jnp.float32)
            ds = (p * (dp - delta)).astype(jnp.bfloat16)
            dq_ref[:, cols] = (jnp.dot(ds, k, preferred_element_type=jnp.float32) * inverse).astype(jnp.bfloat16)
            dk = dk + lax.dot_general(ds, q, (((0,), (0,)), ((), ())), preferred_element_type=jnp.float32)
            dv = dv + lax.dot_general(ph, do, (((0,), (0,)), ((), ())), preferred_element_type=jnp.float32)
            return dk, dv

        zero = jnp.zeros((span, HD), jnp.float32)
        dk, dv = lax.fori_loop(0, group, head, (zero, zero))
        dk_ref[skip:, :] = dk * inverse
        dv_ref[skip:, :] = dv

    first = first_ref[0]
    lower = 0
    for span in spans:
        fits = (first >= full - span) & (first < full - lower)
        pl.when(fits)(functools.partial(run, span))
        lower = span


def attention(query_ids, key_ids, queries, out_grad, window_pair, heads_kv):
    rows, width = queries.shape
    span = window_pair.shape[0]
    group = width // (heads_kv * HD)
    spans = tuple(b * rows for b in (2, 3, 5)) + (span,)
    kernel = functools.partial(attn_kernel, group=group, inverse=1.0 / math.sqrt(HD), spans=spans)
    wide = group * HD
    first = jnp.sum((key_ids < query_ids[0]).astype(jnp.int32)).reshape(1)
    grid_spec = pltpu.PrefetchScalarGridSpec(
        num_scalar_prefetch=1,
        grid=(heads_kv,),
        in_specs=[
            pl.BlockSpec((rows, 1), lambda g, f: (0, 0)),
            pl.BlockSpec((1, span), lambda g, f: (0, 0)),
            pl.BlockSpec((rows, wide), lambda g, f: (0, g)),
            pl.BlockSpec((rows, wide), lambda g, f: (0, g)),
            pl.BlockSpec((span, HD), lambda g, f: (0, g)),
            pl.BlockSpec((span, HD), lambda g, f: (0, heads_kv + g)),
        ],
        out_specs=[
            pl.BlockSpec((rows, wide), lambda g, f: (0, g)),
            pl.BlockSpec((rows, wide), lambda g, f: (0, g)),
            pl.BlockSpec((span, HD), lambda g, f: (0, g)),
            pl.BlockSpec((span, HD), lambda g, f: (0, g)),
        ],
    )
    return pl.pallas_call(
        kernel,
        grid_spec=grid_spec,
        out_shape=[
            jax.ShapeDtypeStruct((rows, width), jnp.bfloat16),
            jax.ShapeDtypeStruct((rows, width), jnp.bfloat16),
            jax.ShapeDtypeStruct((span, heads_kv * HD), jnp.float32),
            jax.ShapeDtypeStruct((span, heads_kv * HD), jnp.float32),
        ],
    )(first, query_ids.reshape(rows, 1), key_ids.reshape(1, span), queries, out_grad, window_pair, window_pair)

def make_shards(n_data, n_cz, n_cw):
    n_context = n_cz * n_cw

    def shards(queries, keys, values, out_grad, layer_input, doc_lens):
        tok_rows = queries.shape[1]
        kv_width = keys.shape[2]
        heads_kv = kv_width // HD
        group = queries.shape[2] // kv_width
        inverse = 1.0 / math.sqrt(HD)
        blocks_back = min(8, n_context // 4)

        owned = D // (n_data * n_context)

        own_pair = jnp.concatenate([keys[0], values[0]], axis=1)
        earlier = [shifted(own_pair, d, n_context) for d in range(blocks_back, 0, -1)]
        window_pair = jnp.concatenate(earlier + [own_pair], axis=0)
        member = lax.axis_index("cw")
        chunks = layer_input[0].reshape(tok_rows, n_data, n_cz, n_cw, owned)
        chunks, window_pair = lax.optimization_barrier((chunks, window_pair))
        chunks = chunks.transpose(3, 0, 2, 1, 4).reshape(n_cw, tok_rows, n_cz * n_data * owned)
        received = [lax.dynamic_index_in_dim(chunks, member, 0, keepdims=False)]
        for k in range(1, n_cw):
            route = [(i, (i + k) % n_cw) for i in range(n_cw)]
            outgoing = lax.dynamic_index_in_dim(chunks, (member + k) % n_cw, 0, keepdims=False)
            received.append(lax.ppermute(outgoing, "cw", route))
        column_share = jnp.concatenate(received[::-1], axis=0)
        span = window_pair.shape[0]
        device = lax.axis_index("cz") * n_cw + lax.axis_index("cw")
        query_pos = device * tok_rows + jnp.arange(tok_rows, dtype=jnp.int32)
        key_pos = (device - blocks_back) * tok_rows + jnp.arange(span, dtype=jnp.int32)
        query_ids = doc_index(doc_lens[0], query_pos)
        key_ids = jnp.where(key_pos >= 0, doc_index(doc_lens[0], key_pos), -1)
        out_half, query_part, key_part, value_part = attention(
            query_ids, key_ids, queries[0], out_grad[0], window_pair, heads_kv
        )
        column_share, key_part, value_part = lax.optimization_barrier(
            (column_share, key_part, value_part)
        )
        grad_scale = 1.0 / math.sqrt(tok_rows * n_context * n_data)

        pair_grad = jnp.concatenate([key_part, value_part], axis=1)

        def block_back(distance):
            first_row = (blocks_back - distance) * tok_rows
            return pair_grad[first_row : first_row + tok_rows]

        total = block_back(0)
        for distance in range(1, blocks_back + 1):
            sent = block_back(distance).astype(jnp.bfloat16)
            total = total + shifted(sent, -distance, n_context).astype(jnp.float32)
        pair_half = total.astype(jnp.bfloat16)
        gathered = [pair_half]
        for k in range(1, n_cw):
            route = [(i, (i + k) % n_cw) for i in range(n_cw)]
            gathered.append(lax.ppermute(pair_half, "cw", route))
        group_grad = jnp.concatenate(gathered[::-1], axis=0)
        batch_grad = lax.dot_general(
            column_share,
            group_grad,
            (((0,), (0,)), ((), ())),
            preferred_element_type=jnp.float32,
        )
        by_layer = lax.psum_scatter(batch_grad * grad_scale, "cz", scatter_dimension=0, tiled=True)
        weight_grad = lax.psum_scatter(by_layer, "dp", scatter_dimension=0, tiled=True)
        attn_out = out_half[None]
        query_grad = query_part[None]
        key_grad = pair_half[:, :kv_width][None]
        value_grad = pair_half[:, kv_width:][None]
        return (attn_out, query_grad, key_grad, value_grad, weight_grad)

    return shards


def solution(mesh):
    n_data = mesh.shape["dp"]
    n_context = mesh.shape["ctx"]
    n_cw = 8 if n_context % 8 == 0 else n_context
    n_cz = n_context // n_cw
    split = Mesh(mesh.devices.reshape(n_data, n_cz, n_cw), ("dp", "cz", "cw"))
    tokens = P("dp", CTX, None)
    in_specs = (tokens, tokens, tokens, tokens, tokens, P("dp", None))
    out_specs = (tokens, tokens, tokens, tokens, P(("dp", "cz", "cw"), None))
    return jax.shard_map(
        make_shards(n_data, n_cz, n_cw),
        mesh=split,
        in_specs=in_specs,
        out_specs=out_specs,
        check_vma=False,
    )
```

```python
import functools
import math

import jax
import jax.numpy as jnp
from jax import lax
from jax.experimental import pallas as pl
from jax.experimental.pallas import tpu as pltpu
from jax.sharding import Mesh
from jax.sharding import PartitionSpec as P

D = 5120
HD = 128


NEGATIVE = -1e30
CTX = ("cz", "cw")


def shifted(block, distance, n_ctx):
    route = [(i - distance, i) for i in range(n_ctx) if 0 <= i - distance < n_ctx]
    return lax.ppermute(block, CTX, route)


def doc_index(lengths_row, positions):
    bounds = jnp.cumsum(lengths_row)
    return jnp.sum((positions[:, None] >= bounds[None, :]).astype(jnp.int32), axis=1)


def attn_kernel(first_ref, qid_ref, kid_ref, q_ref, do_ref, k_ref, v_ref, o_ref, dq_ref, dk_ref, dv_ref, *, group, inverse, spans):
    rows = q_ref.shape[0]
    full = k_ref.shape[0]
    dk_ref[...] = jnp.zeros(dk_ref.shape, dk_ref.dtype)
    dv_ref[...] = jnp.zeros(dv_ref.shape, dv_ref.dtype)

    def run(span):
        skip = full - span
        k = k_ref[skip:, :]
        v = v_ref[skip:, :]
        row = lax.broadcasted_iota(jnp.int32, (rows, span), 0)
        col = lax.broadcasted_iota(jnp.int32, (rows, span), 1)
        allowed = (col <= row + (span - rows)) & (kid_ref[:, skip:] == qid_ref[...])
        def head(h, sums):
            dk, dv = sums
            cols = pl.ds(pl.multiple_of(h * HD, HD), HD)
            q = q_ref[:, cols]
            do = do_ref[:, cols]
            s = lax.dot_general(q, k, (((1,), (1,)), ((), ())), preferred_element_type=jnp.float32) * inverse
            s = jnp.where(allowed, s, NEGATIVE)
            e = jnp.exp(s - jnp.max(s, axis=1, keepdims=True))
            p = e / jnp.sum(e, axis=1, keepdims=True)
            ph = p.astype(jnp.bfloat16)
            oh = jnp.dot(ph, v, preferred_element_type=jnp.float32).astype(jnp.bfloat16)
            o_ref[:, cols] = oh
            delta = jnp.sum(do.astype(jnp.float32) * oh.astype(jnp.float32), axis=1, keepdims=True)
            dp = lax.dot_general(do, v, (((1,), (1,)), ((), ())), preferred_element_type=jnp.float32)
            ds = (p * (dp - delta)).astype(jnp.bfloat16)
            dq_ref[:, cols] = (jnp.dot(ds, k, preferred_element_type=jnp.float32) * inverse).astype(jnp.bfloat16)
            dk = dk + lax.dot_general(ds, q, (((0,), (0,)), ((), ())), preferred_element_type=jnp.float32)
            dv = dv + lax.dot_general(ph, do, (((0,), (0,)), ((), ())), preferred_element_type=jnp.float32)
            return dk, dv

        zero = jnp.zeros((span, HD), jnp.float32)
        dk, dv = lax.fori_loop(0, group, head, (zero, zero))
        dk_ref[skip:, :] = dk * inverse
        dv_ref[skip:, :] = dv

    first = first_ref[0]
    lower = 0
    for span in spans:
        fits = (first >= full - span) & (first < full - lower)
        pl.when(fits)(functools.partial(run, span))
        lower = span


def attention(query_ids, key_ids, queries, out_grad, window_pair, heads_kv):
    rows, width = queries.shape
    span = window_pair.shape[0]
    group = width // (heads_kv * HD)
    spans = tuple(b * rows for b in (2, 3, 5)) + (span,)
    kernel = functools.partial(attn_kernel, group=group, inverse=1.0 / math.sqrt(HD), spans=spans)
    wide = group * HD
    first = jnp.sum((key_ids < query_ids[0]).astype(jnp.int32)).reshape(1)
    grid_spec = pltpu.PrefetchScalarGridSpec(
        num_scalar_prefetch=1,
        grid=(heads_kv,),
        in_specs=[
            pl.BlockSpec((rows, 1), lambda g, f: (0, 0)),
            pl.BlockSpec((1, span), lambda g, f: (0, 0)),
            pl.BlockSpec((rows, wide), lambda g, f: (0, g)),
            pl.BlockSpec((rows, wide), lambda g, f: (0, g)),
            pl.BlockSpec((span, HD), lambda g, f: (0, g)),
            pl.BlockSpec((span, HD), lambda g, f: (0, heads_kv + g)),
        ],
        out_specs=[
            pl.BlockSpec((rows, wide), lambda g, f: (0, g)),
            pl.BlockSpec((rows, wide), lambda g, f: (0, g)),
            pl.BlockSpec((span, HD), lambda g, f: (0, g)),
            pl.BlockSpec((span, HD), lambda g, f: (0, g)),
        ],
    )
    return pl.pallas_call(
        kernel,
        grid_spec=grid_spec,
        out_shape=[
            jax.ShapeDtypeStruct((rows, width), jnp.bfloat16),
            jax.ShapeDtypeStruct((rows, width), jnp.bfloat16),
            jax.ShapeDtypeStruct((span, heads_kv * HD), jnp.float32),
            jax.ShapeDtypeStruct((span, heads_kv * HD), jnp.float32),
        ],
    )(first, query_ids.reshape(rows, 1), key_ids.reshape(1, span), queries, out_grad, window_pair, window_pair)

def make_shards(n_data, n_cz, n_cw):
    n_context = n_cz * n_cw

    def shards(queries, keys, values, out_grad, layer_input, doc_lens):
        tok_rows = queries.shape[1]
        kv_width = keys.shape[2]
        heads_kv = kv_width // HD
        group = queries.shape[2] // kv_width
        inverse = 1.0 / math.sqrt(HD)
        blocks_back = min(8, n_context // 4)

        owned = D // (n_data * n_context)

        own_pair = jnp.concatenate([keys[0], values[0]], axis=1)
        earlier = [shifted(own_pair, d, n_context) for d in range(blocks_back, 0, -1)]
        window_pair = jnp.concatenate(earlier + [own_pair], axis=0)
        span = window_pair.shape[0]
        device = lax.axis_index("cz") * n_cw + lax.axis_index("cw")
        query_pos = device * tok_rows + jnp.arange(tok_rows, dtype=jnp.int32)
        key_pos = (device - blocks_back) * tok_rows + jnp.arange(span, dtype=jnp.int32)
        query_ids = doc_index(doc_lens[0], query_pos)
        key_ids = jnp.where(key_pos >= 0, doc_index(doc_lens[0], key_pos), -1)
        out_half, query_part, key_part, value_part = attention(
            query_ids, key_ids, queries[0], out_grad[0], window_pair, heads_kv
        )
        member = lax.axis_index("cw")
        chunks = layer_input[0].reshape(tok_rows, n_data, n_cz, n_cw, owned)
        chunks, key_part, value_part = lax.optimization_barrier((chunks, key_part, value_part))
        chunks = chunks.transpose(3, 0, 2, 1, 4).reshape(n_cw, tok_rows, n_cz * n_data * owned)
        received = [lax.dynamic_index_in_dim(chunks, member, 0, keepdims=False)]
        for k in range(1, n_cw):
            route = [(i, (i + k) % n_cw) for i in range(n_cw)]
            outgoing = lax.dynamic_index_in_dim(chunks, (member + k) % n_cw, 0, keepdims=False)
            received.append(lax.ppermute(outgoing, "cw", route))
        column_share = jnp.concatenate(received[::-1], axis=0)
        grad_scale = 1.0 / math.sqrt(tok_rows * n_context * n_data)

        pair_grad = jnp.concatenate([key_part, value_part], axis=1)

        def block_back(distance):
            first_row = (blocks_back - distance) * tok_rows
            return pair_grad[first_row : first_row + tok_rows]

        total = block_back(0)
        for distance in range(1, blocks_back + 1):
            sent = block_back(distance).astype(jnp.bfloat16)
            total = total + shifted(sent, -distance, n_context).astype(jnp.float32)
        pair_half = total.astype(jnp.bfloat16)
        gathered = [pair_half]
        for k in range(1, n_cw):
            route = [(i, (i + k) % n_cw) for i in range(n_cw)]
            gathered.append(lax.ppermute(pair_half, "cw", route))
        group_grad = jnp.concatenate(gathered[::-1], axis=0)
        batch_grad = lax.dot_general(
            column_share,
            group_grad,
            (((0,), (0,)), ((), ())),
            preferred_element_type=jnp.float32,
        )
        by_layer = lax.psum_scatter(batch_grad * grad_scale, "cz", scatter_dimension=0, tiled=True)
        weight_grad = lax.psum_scatter(by_layer, "dp", scatter_dimension=0, tiled=True)
        attn_out = out_half[None]
        query_grad = query_part[None]
        key_grad = pair_half[:, :kv_width][None]
        value_grad = pair_half[:, kv_width:][None]
        return (attn_out, query_grad, key_grad, value_grad, weight_grad)

    return shards


def solution(mesh):
    n_data = mesh.shape["dp"]
    n_context = mesh.shape["ctx"]
    n_cw = 8 if n_context % 8 == 0 else n_context
    n_cz = n_context // n_cw
    split = Mesh(mesh.devices.reshape(n_data, n_cz, n_cw), ("dp", "cz", "cw"))
    tokens = P("dp", CTX, None)
    in_specs = (tokens, tokens, tokens, tokens, tokens, P("dp", None))
    out_specs = (tokens, tokens, tokens, tokens, P(("dp", "cz", "cw"), None))
    return jax.shard_map(
        make_shards(n_data, n_cz, n_cw),
        mesh=split,
        in_specs=in_specs,
        out_specs=out_specs,
        check_vma=False,
    )
```

```python
import functools
import math

import jax
import jax.numpy as jnp
from jax import lax
from jax.experimental import pallas as pl
from jax.experimental.pallas import tpu as pltpu
from jax.sharding import Mesh
from jax.sharding import PartitionSpec as P

D = 5120
HD = 128


NEGATIVE = -1e30
CTX = ("cz", "cw")


def shifted(block, distance, n_ctx):
    route = [(i - distance, i) for i in range(n_ctx) if 0 <= i - distance < n_ctx]
    return lax.ppermute(block, CTX, route)


def doc_index(lengths_row, positions):
    bounds = jnp.cumsum(lengths_row)
    return jnp.sum((positions[:, None] >= bounds[None, :]).astype(jnp.int32), axis=1)


def attn_kernel(qid_ref, kid_ref, q_ref, do_ref, k_ref, v_ref, o_ref, dq_ref, dk_ref, dv_ref, *, group, inverse):
    k = k_ref[...]
    v = v_ref[...]
    rows = q_ref.shape[0]
    span = k.shape[0]
    row = lax.broadcasted_iota(jnp.int32, (rows, span), 0)
    col = lax.broadcasted_iota(jnp.int32, (rows, span), 1)
    allowed = (col <= row + (span - rows)) & (kid_ref[...] == qid_ref[...])
    allowed = jnp.concatenate([allowed] * group, axis=0)
    q = jnp.concatenate([q_ref[:, h * HD:(h + 1) * HD] for h in range(group)], axis=0)
    do = jnp.concatenate([do_ref[:, h * HD:(h + 1) * HD] for h in range(group)], axis=0)
    s = lax.dot_general(q, k, (((1,), (1,)), ((), ())), preferred_element_type=jnp.float32) * inverse
    s = jnp.where(allowed, s, NEGATIVE)
    e = jnp.exp(s - jnp.max(s, axis=1, keepdims=True))
    p = e / jnp.sum(e, axis=1, keepdims=True)
    ph = p.astype(jnp.bfloat16)
    oh = jnp.dot(ph, v, preferred_element_type=jnp.float32).astype(jnp.bfloat16)
    delta = jnp.sum(do.astype(jnp.float32) * oh.astype(jnp.float32), axis=1, keepdims=True)
    dp = lax.dot_general(do, v, (((1,), (1,)), ((), ())), preferred_element_type=jnp.float32)
    ds = (p * (dp - delta)).astype(jnp.bfloat16)
    dq = (jnp.dot(ds, k, preferred_element_type=jnp.float32) * inverse).astype(jnp.bfloat16)
    for h in range(group):
        o_ref[:, h * HD:(h + 1) * HD] = oh[h * rows:(h + 1) * rows]
        dq_ref[:, h * HD:(h + 1) * HD] = dq[h * rows:(h + 1) * rows]
    dk_ref[...] = lax.dot_general(ds, q, (((0,), (0,)), ((), ())), preferred_element_type=jnp.float32) * inverse
    dv_ref[...] = lax.dot_general(ph, do, (((0,), (0,)), ((), ())), preferred_element_type=jnp.float32)


def attention(query_ids, key_ids, queries, out_grad, window_pair, heads_kv):
    rows, width = queries.shape
    span = window_pair.shape[0]
    group = width // (heads_kv * HD)
    kernel = functools.partial(attn_kernel, group=group, inverse=1.0 / math.sqrt(HD))
    wide = group * HD
    return pl.pallas_call(
        kernel,
        grid=(heads_kv,),
        in_specs=[
            pl.BlockSpec((rows, 1), lambda g: (0, 0)),
            pl.BlockSpec((1, span), lambda g: (0, 0)),
            pl.BlockSpec((rows, wide), lambda g: (0, g)),
            pl.BlockSpec((rows, wide), lambda g: (0, g)),
            pl.BlockSpec((span, HD), lambda g: (0, g)),
            pl.BlockSpec((span, HD), lambda g: (0, heads_kv + g)),
        ],
        out_specs=[
            pl.BlockSpec((rows, wide), lambda g: (0, g)),
            pl.BlockSpec((rows, wide), lambda g: (0, g)),
            pl.BlockSpec((span, HD), lambda g: (0, g)),
            pl.BlockSpec((span, HD), lambda g: (0, g)),
        ],
        out_shape=[
            jax.ShapeDtypeStruct((rows, width), jnp.bfloat16),
            jax.ShapeDtypeStruct((rows, width), jnp.bfloat16),
            jax.ShapeDtypeStruct((span, heads_kv * HD), jnp.float32),
            jax.ShapeDtypeStruct((span, heads_kv * HD), jnp.float32),
        ],
        compiler_params=pltpu.CompilerParams(vmem_limit_bytes=56 * 1024 * 1024),
    )(query_ids.reshape(rows, 1), key_ids.reshape(1, span), queries, out_grad, window_pair, window_pair)

def make_shards(n_data, n_cz, n_cw):
    n_context = n_cz * n_cw

    def shards(queries, keys, values, out_grad, layer_input, doc_lens):
        tok_rows = queries.shape[1]
        kv_width = keys.shape[2]
        heads_kv = kv_width // HD
        group = queries.shape[2] // kv_width
        inverse = 1.0 / math.sqrt(HD)
        blocks_back = min(8, n_context // 4)

        owned = D // (n_data * n_context)

        own_pair = jnp.concatenate([keys[0], values[0]], axis=1)
        earlier = [shifted(own_pair, d, n_context) for d in range(blocks_back, 0, -1)]
        window_pair = jnp.concatenate(earlier + [own_pair], axis=0)
        member = lax.axis_index("cw")
        chunks = layer_input[0].reshape(tok_rows, n_data, n_cz, n_cw, owned)
        chunks, window_pair = lax.optimization_barrier((chunks, window_pair))
        chunks = chunks.transpose(3, 0, 2, 1, 4).reshape(n_cw, tok_rows, n_cz * n_data * owned)
        received = [lax.dynamic_index_in_dim(chunks, member, 0, keepdims=False)]
        for k in range(1, n_cw):
            route = [(i, (i + k) % n_cw) for i in range(n_cw)]
            outgoing = lax.dynamic_index_in_dim(chunks, (member + k) % n_cw, 0, keepdims=False)
            received.append(lax.ppermute(outgoing, "cw", route))
        column_share = jnp.concatenate(received[::-1], axis=0)
        span = window_pair.shape[0]
        device = lax.axis_index("cz") * n_cw + lax.axis_index("cw")
        query_pos = device * tok_rows + jnp.arange(tok_rows, dtype=jnp.int32)
        key_pos = (device - blocks_back) * tok_rows + jnp.arange(span, dtype=jnp.int32)
        query_ids = doc_index(doc_lens[0], query_pos)
        key_ids = jnp.where(key_pos >= 0, doc_index(doc_lens[0], key_pos), -1)
        out_half, query_part, key_part, value_part = attention(
            query_ids, key_ids, queries[0], out_grad[0], window_pair, heads_kv
        )
        column_share, key_part, value_part = lax.optimization_barrier(
            (column_share, key_part, value_part)
        )
        grad_scale = 1.0 / math.sqrt(tok_rows * n_context * n_data)

        pair_grad = jnp.concatenate([key_part, value_part], axis=1)

        def block_back(distance):
            first_row = (blocks_back - distance) * tok_rows
            return pair_grad[first_row : first_row + tok_rows]

        total = block_back(0)
        for distance in range(1, blocks_back + 1):
            sent = block_back(distance).astype(jnp.bfloat16)
            total = total + shifted(sent, -distance, n_context).astype(jnp.float32)
        pair_half = total.astype(jnp.bfloat16)
        gathered = [pair_half]
        for k in range(1, n_cw):
            route = [(i, (i + k) % n_cw) for i in range(n_cw)]
            gathered.append(lax.ppermute(pair_half, "cw", route))
        group_grad = jnp.concatenate(gathered[::-1], axis=0)
        batch_grad = lax.dot_general(
            column_share,
            group_grad,
            (((0,), (0,)), ((), ())),
            preferred_element_type=jnp.float32,
        )
        by_layer = lax.psum_scatter(batch_grad * grad_scale, "cz", scatter_dimension=0, tiled=True)
        weight_grad = lax.psum_scatter(by_layer, "dp", scatter_dimension=0, tiled=True)
        attn_out = out_half[None]
        query_grad = query_part[None]
        key_grad = pair_half[:, :kv_width][None]
        value_grad = pair_half[:, kv_width:][None]
        return (attn_out, query_grad, key_grad, value_grad, weight_grad)

    return shards


def solution(mesh):
    n_data = mesh.shape["dp"]
    n_context = mesh.shape["ctx"]
    n_cw = 8 if n_context % 8 == 0 else n_context
    n_cz = n_context // n_cw
    split = Mesh(mesh.devices.reshape(n_data, n_cz, n_cw), ("dp", "cz", "cw"))
    tokens = P("dp", CTX, None)
    in_specs = (tokens, tokens, tokens, tokens, tokens, P("dp", None))
    out_specs = (tokens, tokens, tokens, tokens, P(("dp", "cz", "cw"), None))
    return jax.shard_map(
        make_shards(n_data, n_cz, n_cw),
        mesh=split,
        in_specs=in_specs,
        out_specs=out_specs,
        check_vma=False,
    )
```

```python
import functools
import math

import jax
import jax.numpy as jnp
from jax import lax
from jax.experimental import pallas as pl
from jax.experimental.pallas import tpu as pltpu
from jax.sharding import Mesh
from jax.sharding import PartitionSpec as P

D = 5120
HD = 128


NEGATIVE = -1e30
CTX = ("cz", "cw")


def shifted(block, distance, n_ctx):
    route = [(i - distance, i) for i in range(n_ctx) if 0 <= i - distance < n_ctx]
    return lax.ppermute(block, CTX, route)


def doc_index(lengths_row, positions):
    bounds = jnp.cumsum(lengths_row)
    return jnp.sum((positions[:, None] >= bounds[None, :]).astype(jnp.int32), axis=1)


def attn_kernel(qid_ref, kid_ref, q_ref, do_ref, *refs, group, inverse, blocks):
    k_refs, v_refs = refs[:blocks], refs[blocks:2 * blocks]
    o_ref, dq_ref, dk_ref, dv_ref = refs[2 * blocks:]
    k = jnp.concatenate([r[...] for r in k_refs], axis=0)
    v = jnp.concatenate([r[...] for r in v_refs], axis=0)
    rows = q_ref.shape[0]
    span = k.shape[0]
    row = lax.broadcasted_iota(jnp.int32, (rows, span), 0)
    col = lax.broadcasted_iota(jnp.int32, (rows, span), 1)
    allowed = (col <= row + (span - rows)) & (kid_ref[...] == qid_ref[...])
    allowed = jnp.concatenate([allowed] * group, axis=0)
    q = jnp.concatenate([q_ref[:, h * HD:(h + 1) * HD] for h in range(group)], axis=0)
    do = jnp.concatenate([do_ref[:, h * HD:(h + 1) * HD] for h in range(group)], axis=0)
    s = lax.dot_general(q, k, (((1,), (1,)), ((), ())), preferred_element_type=jnp.float32) * inverse
    s = jnp.where(allowed, s, NEGATIVE)
    e = jnp.exp(s - jnp.max(s, axis=1, keepdims=True))
    p = e / jnp.sum(e, axis=1, keepdims=True)
    ph = p.astype(jnp.bfloat16)
    oh = jnp.dot(ph, v, preferred_element_type=jnp.float32).astype(jnp.bfloat16)
    delta = jnp.sum(do.astype(jnp.float32) * oh.astype(jnp.float32), axis=1, keepdims=True)
    dp = lax.dot_general(do, v, (((1,), (1,)), ((), ())), preferred_element_type=jnp.float32)
    ds = (p * (dp - delta)).astype(jnp.bfloat16)
    dq = (jnp.dot(ds, k, preferred_element_type=jnp.float32) * inverse).astype(jnp.bfloat16)
    for h in range(group):
        o_ref[:, h * HD:(h + 1) * HD] = oh[h * rows:(h + 1) * rows]
        dq_ref[:, h * HD:(h + 1) * HD] = dq[h * rows:(h + 1) * rows]
    dk_ref[...] = lax.dot_general(ds, q, (((0,), (0,)), ((), ())), preferred_element_type=jnp.float32) * inverse
    dv_ref[...] = lax.dot_general(ph, do, (((0,), (0,)), ((), ())), preferred_element_type=jnp.float32)


def attention(query_ids, key_ids, queries, out_grad, window_blocks, heads_kv):
    rows, width = queries.shape
    blocks = len(window_blocks)
    span = blocks * rows
    group = width // (heads_kv * HD)
    kernel = functools.partial(attn_kernel, group=group, inverse=1.0 / math.sqrt(HD), blocks=blocks)
    wide = group * HD
    key_specs = [pl.BlockSpec((rows, HD), lambda g: (0, g)) for _ in range(blocks)]
    value_specs = [pl.BlockSpec((rows, HD), lambda g: (0, heads_kv + g)) for _ in range(blocks)]
    return pl.pallas_call(
        kernel,
        grid=(heads_kv,),
        in_specs=[
            pl.BlockSpec((rows, 1), lambda g: (0, 0)),
            pl.BlockSpec((1, span), lambda g: (0, 0)),
            pl.BlockSpec((rows, wide), lambda g: (0, g)),
            pl.BlockSpec((rows, wide), lambda g: (0, g)),
        ]
        + key_specs
        + value_specs,
        out_specs=[
            pl.BlockSpec((rows, wide), lambda g: (0, g)),
            pl.BlockSpec((rows, wide), lambda g: (0, g)),
            pl.BlockSpec((span, HD), lambda g: (0, g)),
            pl.BlockSpec((span, HD), lambda g: (0, g)),
        ],
        out_shape=[
            jax.ShapeDtypeStruct((rows, width), jnp.bfloat16),
            jax.ShapeDtypeStruct((rows, width), jnp.bfloat16),
            jax.ShapeDtypeStruct((span, heads_kv * HD), jnp.float32),
            jax.ShapeDtypeStruct((span, heads_kv * HD), jnp.float32),
        ],
        compiler_params=pltpu.CompilerParams(vmem_limit_bytes=56 * 1024 * 1024),
    )(query_ids.reshape(rows, 1), key_ids.reshape(1, span), queries, out_grad, *window_blocks, *window_blocks)


def make_shards(n_data, n_cz, n_cw):
    n_context = n_cz * n_cw

    def shards(queries, keys, values, out_grad, layer_input, doc_lens):
        tok_rows = queries.shape[1]
        kv_width = keys.shape[2]
        heads_kv = kv_width // HD
        group = queries.shape[2] // kv_width
        inverse = 1.0 / math.sqrt(HD)
        blocks_back = min(8, n_context // 4)

        owned = D // (n_data * n_context)

        own_pair = jnp.concatenate([keys[0], values[0]], axis=1)
        earlier = [shifted(own_pair, d, n_context) for d in range(blocks_back, 0, -1)]
        window_blocks = earlier + [own_pair]
        member = lax.axis_index("cw")
        chunks = layer_input[0].reshape(tok_rows, n_data, n_cz, n_cw, owned)
        chunks, window_blocks = lax.optimization_barrier((chunks, window_blocks))
        chunks = chunks.transpose(3, 0, 2, 1, 4).reshape(n_cw, tok_rows, n_cz * n_data * owned)
        received = [lax.dynamic_index_in_dim(chunks, member, 0, keepdims=False)]
        for k in range(1, n_cw):
            route = [(i, (i + k) % n_cw) for i in range(n_cw)]
            outgoing = lax.dynamic_index_in_dim(chunks, (member + k) % n_cw, 0, keepdims=False)
            received.append(lax.ppermute(outgoing, "cw", route))
        column_share = jnp.concatenate(received[::-1], axis=0)
        span = len(window_blocks) * tok_rows
        device = lax.axis_index("cz") * n_cw + lax.axis_index("cw")
        query_pos = device * tok_rows + jnp.arange(tok_rows, dtype=jnp.int32)
        key_pos = (device - blocks_back) * tok_rows + jnp.arange(span, dtype=jnp.int32)
        query_ids = doc_index(doc_lens[0], query_pos)
        key_ids = jnp.where(key_pos >= 0, doc_index(doc_lens[0], key_pos), -1)
        out_half, query_part, key_part, value_part = attention(
            query_ids, key_ids, queries[0], out_grad[0], window_blocks, heads_kv
        )
        column_share, key_part, value_part = lax.optimization_barrier(
            (column_share, key_part, value_part)
        )
        grad_scale = 1.0 / math.sqrt(tok_rows * n_context * n_data)

        pair_grad = jnp.concatenate([key_part, value_part], axis=1)

        def block_back(distance):
            first_row = (blocks_back - distance) * tok_rows
            return pair_grad[first_row : first_row + tok_rows]

        total = block_back(0)
        for distance in range(1, blocks_back + 1):
            sent = block_back(distance).astype(jnp.bfloat16)
            total = total + shifted(sent, -distance, n_context).astype(jnp.float32)
        pair_half = total.astype(jnp.bfloat16)
        gathered = [pair_half]
        for k in range(1, n_cw):
            route = [(i, (i + k) % n_cw) for i in range(n_cw)]
            gathered.append(lax.ppermute(pair_half, "cw", route))
        group_grad = jnp.concatenate(gathered[::-1], axis=0)
        batch_grad = lax.dot_general(
            column_share,
            group_grad,
            (((0,), (0,)), ((), ())),
            preferred_element_type=jnp.float32,
        )
        by_layer = lax.psum_scatter(batch_grad * grad_scale, "cz", scatter_dimension=0, tiled=True)
        weight_grad = lax.psum_scatter(by_layer, "dp", scatter_dimension=0, tiled=True)
        attn_out = out_half[None]
        query_grad = query_part[None]
        key_grad = pair_half[:, :kv_width][None]
        value_grad = pair_half[:, kv_width:][None]
        return (attn_out, query_grad, key_grad, value_grad, weight_grad)

    return shards


def solution(mesh):
    n_data = mesh.shape["dp"]
    n_context = mesh.shape["ctx"]
    n_cw = 8 if n_context % 8 == 0 else n_context
    n_cz = n_context // n_cw
    split = Mesh(mesh.devices.reshape(n_data, n_cz, n_cw), ("dp", "cz", "cw"))
    tokens = P("dp", CTX, None)
    in_specs = (tokens, tokens, tokens, tokens, tokens, P("dp", None))
    out_specs = (tokens, tokens, tokens, tokens, P(("dp", "cz", "cw"), None))
    return jax.shard_map(
        make_shards(n_data, n_cz, n_cw),
        mesh=split,
        in_specs=in_specs,
        out_specs=out_specs,
        check_vma=False,
    )
```

```python
import functools
import math

import jax
import jax.numpy as jnp
from jax import lax
from jax.experimental import pallas as pl
from jax.experimental.pallas import tpu as pltpu
from jax.sharding import Mesh
from jax.sharding import PartitionSpec as P

D = 5120
HD = 128


NEGATIVE = -1e30
CTX = ("cz", "cw")


def shifted(block, distance, n_ctx):
    route = [(i - distance, i) for i in range(n_ctx) if 0 <= i - distance < n_ctx]
    return lax.ppermute(block, CTX, route)


def doc_index(lengths_row, positions):
    bounds = jnp.cumsum(lengths_row)
    return jnp.sum((positions[:, None] >= bounds[None, :]).astype(jnp.int32), axis=1)


def attn_kernel(qid_ref, kid_ref, q_ref, do_ref, *refs, group, inverse, blocks):
    k_refs, v_refs = refs[:blocks], refs[blocks:2 * blocks]
    o_ref, dq_ref, dk_ref, dv_ref = refs[2 * blocks:]
    k = jnp.concatenate([r[...] for r in k_refs], axis=0)
    v = jnp.concatenate([r[...] for r in v_refs], axis=0)
    rows = q_ref.shape[0]
    span = k.shape[0]
    row = lax.broadcasted_iota(jnp.int32, (rows, span), 0)
    col = lax.broadcasted_iota(jnp.int32, (rows, span), 1)
    allowed = (col <= row + (span - rows)) & (kid_ref[...] == qid_ref[...])
    allowed = jnp.concatenate([allowed] * group, axis=0)
    q = jnp.concatenate([q_ref[:, h * HD:(h + 1) * HD] for h in range(group)], axis=0)
    do = jnp.concatenate([do_ref[:, h * HD:(h + 1) * HD] for h in range(group)], axis=0)
    s = lax.dot_general(q, k, (((1,), (1,)), ((), ())), preferred_element_type=jnp.float32) * inverse
    s = jnp.where(allowed, s, NEGATIVE)
    e = jnp.exp(s - jnp.max(s, axis=1, keepdims=True))
    p = e / jnp.sum(e, axis=1, keepdims=True)
    ph = p.astype(jnp.bfloat16)
    oh = jnp.dot(ph, v, preferred_element_type=jnp.float32).astype(jnp.bfloat16)
    delta = jnp.sum(do.astype(jnp.float32) * oh.astype(jnp.float32), axis=1, keepdims=True)
    dp = lax.dot_general(do, v, (((1,), (1,)), ((), ())), preferred_element_type=jnp.float32)
    ds = (p * (dp - delta)).astype(jnp.bfloat16)
    dq = (jnp.dot(ds, k, preferred_element_type=jnp.float32) * inverse).astype(jnp.bfloat16)
    for h in range(group):
        o_ref[:, h * HD:(h + 1) * HD] = oh[h * rows:(h + 1) * rows]
        dq_ref[:, h * HD:(h + 1) * HD] = dq[h * rows:(h + 1) * rows]
    dk_ref[...] = lax.dot_general(ds, q, (((0,), (0,)), ((), ())), preferred_element_type=jnp.float32) * inverse
    dv_ref[...] = lax.dot_general(ph, do, (((0,), (0,)), ((), ())), preferred_element_type=jnp.float32)


def attention(query_ids, key_ids, queries, out_grad, window_blocks, heads_kv):
    rows, width = queries.shape
    blocks = len(window_blocks)
    span = blocks * rows
    group = width // (heads_kv * HD)
    kernel = functools.partial(attn_kernel, group=group, inverse=1.0 / math.sqrt(HD), blocks=blocks)
    wide = group * HD
    key_specs = [pl.BlockSpec((rows, HD), lambda g: (0, g)) for _ in range(blocks)]
    value_specs = [pl.BlockSpec((rows, HD), lambda g: (0, heads_kv + g)) for _ in range(blocks)]
    return pl.pallas_call(
        kernel,
        grid=(heads_kv,),
        in_specs=[
            pl.BlockSpec((rows, 1), lambda g: (0, 0)),
            pl.BlockSpec((1, span), lambda g: (0, 0)),
            pl.BlockSpec((rows, wide), lambda g: (0, g)),
            pl.BlockSpec((rows, wide), lambda g: (0, g)),
        ]
        + key_specs
        + value_specs,
        out_specs=[
            pl.BlockSpec((rows, wide), lambda g: (0, g)),
            pl.BlockSpec((rows, wide), lambda g: (0, g)),
            pl.BlockSpec((span, HD), lambda g: (0, g)),
            pl.BlockSpec((span, HD), lambda g: (0, g)),
        ],
        out_shape=[
            jax.ShapeDtypeStruct((rows, width), jnp.bfloat16),
            jax.ShapeDtypeStruct((rows, width), jnp.bfloat16),
            jax.ShapeDtypeStruct((span, heads_kv * HD), jnp.float32),
            jax.ShapeDtypeStruct((span, heads_kv * HD), jnp.float32),
        ],
        compiler_params=pltpu.CompilerParams(vmem_limit_bytes=56 * 1024 * 1024),
    )(query_ids.reshape(rows, 1), key_ids.reshape(1, span), queries, out_grad, *window_blocks, *window_blocks)


def make_shards(n_data, n_cz, n_cw):
    n_context = n_cz * n_cw

    def shards(queries, keys, values, out_grad, layer_input, doc_lens):
        tok_rows = queries.shape[1]
        kv_width = keys.shape[2]
        heads_kv = kv_width // HD
        group = queries.shape[2] // kv_width
        inverse = 1.0 / math.sqrt(HD)
        blocks_back = min(8, n_context // 4)

        owned = D // (n_data * n_context)

        own_pair = jnp.concatenate([keys[0], values[0]], axis=1)
        earlier = [shifted(own_pair, d, n_context) for d in range(blocks_back, 0, -1)]
        window_blocks = earlier + [own_pair]
        member = lax.axis_index("cw")
        chunks = layer_input[0].reshape(tok_rows, n_data, n_cz, n_cw, owned)
        chunks, window_blocks = lax.optimization_barrier((chunks, window_blocks))
        chunks = chunks.transpose(3, 0, 2, 1, 4).reshape(n_cw, tok_rows, n_cz * n_data * owned)
        received = [lax.dynamic_index_in_dim(chunks, member, 0, keepdims=False)]
        for k in range(1, n_cw):
            route = [(i, (i + k) % n_cw) for i in range(n_cw)]
            outgoing = lax.dynamic_index_in_dim(chunks, (member + k) % n_cw, 0, keepdims=False)
            received.append(lax.ppermute(outgoing, "cw", route))
        column_share = jnp.concatenate(received[::-1], axis=0)
        span = len(window_blocks) * tok_rows
        device = lax.axis_index("cz") * n_cw + lax.axis_index("cw")
        query_pos = device * tok_rows + jnp.arange(tok_rows, dtype=jnp.int32)
        key_pos = (device - blocks_back) * tok_rows + jnp.arange(span, dtype=jnp.int32)
        query_ids = doc_index(doc_lens[0], query_pos)
        key_ids = jnp.where(key_pos >= 0, doc_index(doc_lens[0], key_pos), -1)
        out_half, query_part, key_part, value_part = attention(
            query_ids, key_ids, queries[0], out_grad[0], window_blocks, heads_kv
        )
        column_share, key_part, value_part = lax.optimization_barrier(
            (column_share, key_part, value_part)
        )
        grad_scale = 1.0 / math.sqrt(tok_rows * n_context * n_data)

        pair_grad = jnp.concatenate([key_part, value_part], axis=1)

        def block_back(distance):
            first_row = (blocks_back - distance) * tok_rows
            return pair_grad[first_row : first_row + tok_rows]

        total = block_back(0)
        for distance in range(1, blocks_back + 1):
            sent = block_back(distance).astype(jnp.bfloat16)
            total = total + shifted(sent, -distance, n_context).astype(jnp.float32)
        pair_half = total.astype(jnp.bfloat16)
        group_grad = lax.all_gather(pair_half, "cw", axis=0, tiled=True)
        group_grad = lax.dynamic_slice_in_dim(
            jnp.concatenate([group_grad, group_grad], axis=0),
            ((member + 1) % n_cw) * tok_rows,
            n_cw * tok_rows,
            0,
        )
        batch_grad = lax.dot_general(
            column_share,
            group_grad,
            (((0,), (0,)), ((), ())),
            preferred_element_type=jnp.float32,
        )
        by_layer = lax.psum_scatter(batch_grad * grad_scale, "cz", scatter_dimension=0, tiled=True)
        weight_grad = lax.psum_scatter(by_layer, "dp", scatter_dimension=0, tiled=True)
        attn_out = out_half[None]
        query_grad = query_part[None]
        key_grad = pair_half[:, :kv_width][None]
        value_grad = pair_half[:, kv_width:][None]
        return (attn_out, query_grad, key_grad, value_grad, weight_grad)

    return shards


def solution(mesh):
    n_data = mesh.shape["dp"]
    n_context = mesh.shape["ctx"]
    n_cw = 8 if n_context % 8 == 0 else n_context
    n_cz = n_context // n_cw
    split = Mesh(mesh.devices.reshape(n_data, n_cz, n_cw), ("dp", "cz", "cw"))
    tokens = P("dp", CTX, None)
    in_specs = (tokens, tokens, tokens, tokens, tokens, P("dp", None))
    out_specs = (tokens, tokens, tokens, tokens, P(("dp", "cz", "cw"), None))
    return jax.shard_map(
        make_shards(n_data, n_cz, n_cw),
        mesh=split,
        in_specs=in_specs,
        out_specs=out_specs,
        check_vma=False,
    )
```

```python
import functools
import math

import jax
import jax.numpy as jnp
from jax import lax
from jax.experimental import pallas as pl
from jax.experimental.pallas import tpu as pltpu
from jax.sharding import Mesh
from jax.sharding import PartitionSpec as P

D = 5120
HD = 128


NEGATIVE = -1e30
CTX = ("cz", "cw")


def shifted(block, distance, n_ctx):
    route = [(i - distance, i) for i in range(n_ctx) if 0 <= i - distance < n_ctx]
    return lax.ppermute(block, CTX, route)


def doc_index(lengths_row, positions):
    bounds = jnp.cumsum(lengths_row)
    return jnp.sum((positions[:, None] >= bounds[None, :]).astype(jnp.int32), axis=1)


def attn_kernel(qid_ref, kid_ref, q_ref, do_ref, *refs, group, inverse, blocks):
    k_refs, v_refs = refs[:blocks], refs[blocks:2 * blocks]
    o_ref, dq_ref, dk_ref, dv_ref = refs[2 * blocks:]
    k = jnp.concatenate([r[...] for r in k_refs], axis=0)
    v = jnp.concatenate([r[...] for r in v_refs], axis=0)
    rows = q_ref.shape[0]
    span = k.shape[0]
    row = lax.broadcasted_iota(jnp.int32, (rows, span), 0)
    col = lax.broadcasted_iota(jnp.int32, (rows, span), 1)
    allowed = (col <= row + (span - rows)) & (kid_ref[...] == qid_ref[...])
    allowed = jnp.concatenate([allowed] * group, axis=0)
    q = jnp.concatenate([q_ref[:, h * HD:(h + 1) * HD] for h in range(group)], axis=0)
    do = jnp.concatenate([do_ref[:, h * HD:(h + 1) * HD] for h in range(group)], axis=0)
    s = lax.dot_general(q, k, (((1,), (1,)), ((), ())), preferred_element_type=jnp.float32) * inverse
    s = jnp.where(allowed, s, NEGATIVE)
    e = jnp.exp(s - jnp.max(s, axis=1, keepdims=True))
    p = e / jnp.sum(e, axis=1, keepdims=True)
    ph = p.astype(jnp.bfloat16)
    oh = jnp.dot(ph, v, preferred_element_type=jnp.float32).astype(jnp.bfloat16)
    delta = jnp.sum(do.astype(jnp.float32) * oh.astype(jnp.float32), axis=1, keepdims=True)
    dp = lax.dot_general(do, v, (((1,), (1,)), ((), ())), preferred_element_type=jnp.float32)
    ds = (p * (dp - delta)).astype(jnp.bfloat16)
    dq = (jnp.dot(ds, k, preferred_element_type=jnp.float32) * inverse).astype(jnp.bfloat16)
    for h in range(group):
        o_ref[:, h * HD:(h + 1) * HD] = oh[h * rows:(h + 1) * rows]
        dq_ref[:, h * HD:(h + 1) * HD] = dq[h * rows:(h + 1) * rows]
    dk_ref[...] = lax.dot_general(ds, q, (((0,), (0,)), ((), ())), preferred_element_type=jnp.float32) * inverse
    dv_ref[...] = lax.dot_general(ph, do, (((0,), (0,)), ((), ())), preferred_element_type=jnp.float32)


def attention(query_ids, key_ids, queries, out_grad, window_blocks, heads_kv):
    rows, width = queries.shape
    blocks = len(window_blocks)
    span = blocks * rows
    group = width // (heads_kv * HD)
    kernel = functools.partial(attn_kernel, group=group, inverse=1.0 / math.sqrt(HD), blocks=blocks)
    wide = group * HD
    key_specs = [pl.BlockSpec((rows, HD), lambda g: (0, g)) for _ in range(blocks)]
    value_specs = [pl.BlockSpec((rows, HD), lambda g: (0, heads_kv + g)) for _ in range(blocks)]
    return pl.pallas_call(
        kernel,
        grid=(heads_kv,),
        in_specs=[
            pl.BlockSpec((rows, 1), lambda g: (0, 0)),
            pl.BlockSpec((1, span), lambda g: (0, 0)),
            pl.BlockSpec((rows, wide), lambda g: (0, g)),
            pl.BlockSpec((rows, wide), lambda g: (0, g)),
        ]
        + key_specs
        + value_specs,
        out_specs=[
            pl.BlockSpec((rows, wide), lambda g: (0, g)),
            pl.BlockSpec((rows, wide), lambda g: (0, g)),
            pl.BlockSpec((span, HD), lambda g: (0, g)),
            pl.BlockSpec((span, HD), lambda g: (0, g)),
        ],
        out_shape=[
            jax.ShapeDtypeStruct((rows, width), jnp.bfloat16),
            jax.ShapeDtypeStruct((rows, width), jnp.bfloat16),
            jax.ShapeDtypeStruct((span, heads_kv * HD), jnp.float32),
            jax.ShapeDtypeStruct((span, heads_kv * HD), jnp.float32),
        ],
        compiler_params=pltpu.CompilerParams(vmem_limit_bytes=56 * 1024 * 1024),
    )(query_ids.reshape(rows, 1), key_ids.reshape(1, span), queries, out_grad, *window_blocks, *window_blocks)


def make_shards(n_data, n_cz, n_cw):
    n_context = n_cz * n_cw

    def shards(queries, keys, values, out_grad, layer_input, doc_lens):
        tok_rows = queries.shape[1]
        kv_width = keys.shape[2]
        heads_kv = kv_width // HD
        group = queries.shape[2] // kv_width
        inverse = 1.0 / math.sqrt(HD)
        blocks_back = min(8, n_context // 4)

        owned = D // (n_data * n_context)

        own_pair = jnp.concatenate([keys[0], values[0]], axis=1)
        earlier = [shifted(own_pair, d, n_context) for d in range(blocks_back, 0, -1)]
        window_blocks = earlier + [own_pair]
        member = lax.axis_index("cw")
        chunks = layer_input[0].reshape(tok_rows, n_data, n_cz, n_cw, owned)
        chunks, window_blocks = lax.optimization_barrier((chunks, window_blocks))
        chunks = chunks.transpose(3, 0, 2, 1, 4).reshape(n_cw, tok_rows, n_cz * n_data * owned)
        received = [lax.dynamic_index_in_dim(chunks, member, 0, keepdims=False)]
        for k in range(1, n_cw):
            route = [(i, (i + k) % n_cw) for i in range(n_cw)]
            outgoing = lax.dynamic_index_in_dim(chunks, (member + k) % n_cw, 0, keepdims=False)
            received.append(lax.ppermute(outgoing, "cw", route))
        column_share = jnp.concatenate(received[::-1], axis=0)
        span = len(window_blocks) * tok_rows
        device = lax.axis_index("cz") * n_cw + lax.axis_index("cw")
        query_pos = device * tok_rows + jnp.arange(tok_rows, dtype=jnp.int32)
        key_pos = (device - blocks_back) * tok_rows + jnp.arange(span, dtype=jnp.int32)
        query_ids = doc_index(doc_lens[0], query_pos)
        key_ids = jnp.where(key_pos >= 0, doc_index(doc_lens[0], key_pos), -1)
        out_half, query_part, key_part, value_part = attention(
            query_ids, key_ids, queries[0], out_grad[0], window_blocks, heads_kv
        )
        column_share, key_part, value_part = lax.optimization_barrier(
            (column_share, key_part, value_part)
        )
        grad_scale = 1.0 / math.sqrt(tok_rows * n_context * n_data)

        pair_grad = jnp.concatenate([key_part, value_part], axis=1)

        def block_back(distance):
            first_row = (blocks_back - distance) * tok_rows
            return pair_grad[first_row : first_row + tok_rows]

        total = block_back(0)
        for distance in range(1, blocks_back + 1):
            sent = block_back(distance).astype(jnp.bfloat16)
            total = total + shifted(sent, -distance, n_context).astype(jnp.float32)
        pair_half = total.astype(jnp.bfloat16)
        gathered = [pair_half]
        for k in range(1, n_cw):
            route = [(i, (i + k) % n_cw) for i in range(n_cw)]
            gathered.append(lax.ppermute(pair_half, "cw", route))
        group_grad = jnp.concatenate(gathered[::-1], axis=0)
        batch_grad = lax.dot_general(
            column_share,
            group_grad,
            (((0,), (0,)), ((), ())),
            preferred_element_type=jnp.float32,
        )
        by_layer = lax.psum_scatter(batch_grad * grad_scale, "cz", scatter_dimension=0, tiled=True)
        by_layer = by_layer.reshape(n_data, owned * 2 * kv_width // 128, 128)
        weight_grad = lax.psum_scatter(by_layer, "dp", scatter_dimension=0, tiled=True)
        weight_grad = weight_grad.reshape(owned, 2 * kv_width)
        attn_out = out_half[None]
        query_grad = query_part[None]
        key_grad = pair_half[:, :kv_width][None]
        value_grad = pair_half[:, kv_width:][None]
        return (attn_out, query_grad, key_grad, value_grad, weight_grad)

    return shards


def solution(mesh):
    n_data = mesh.shape["dp"]
    n_context = mesh.shape["ctx"]
    n_cw = 8 if n_context % 8 == 0 else n_context
    n_cz = n_context // n_cw
    split = Mesh(mesh.devices.reshape(n_data, n_cz, n_cw), ("dp", "cz", "cw"))
    tokens = P("dp", CTX, None)
    in_specs = (tokens, tokens, tokens, tokens, tokens, P("dp", None))
    out_specs = (tokens, tokens, tokens, tokens, P(("dp", "cz", "cw"), None))
    return jax.shard_map(
        make_shards(n_data, n_cz, n_cw),
        mesh=split,
        in_specs=in_specs,
        out_specs=out_specs,
        check_vma=False,
    )
```

```python
import functools
import math

import jax
import jax.numpy as jnp
from jax import lax
from jax.experimental import pallas as pl
from jax.experimental.pallas import tpu as pltpu
from jax.sharding import Mesh
from jax.sharding import PartitionSpec as P

D = 5120
HD = 128


NEGATIVE = -1e30
CTX = ("cz", "cw")


def shifted(block, distance, n_ctx):
    route = [(i - distance, i) for i in range(n_ctx) if 0 <= i - distance < n_ctx]
    return lax.ppermute(block, CTX, route)


def doc_index(lengths_row, positions):
    bounds = jnp.cumsum(lengths_row)
    return jnp.sum((positions[:, None] >= bounds[None, :]).astype(jnp.int32), axis=1)


def attn_kernel(qid_ref, kid_ref, q_ref, do_ref, *refs, group, inverse, blocks):
    k_refs, v_refs = refs[:blocks], refs[blocks:2 * blocks]
    o_ref, dq_ref, dk_ref, dv_ref = refs[2 * blocks:]
    k = jnp.concatenate([r[...] for r in k_refs], axis=0)
    v = jnp.concatenate([r[...] for r in v_refs], axis=0)
    rows = q_ref.shape[0]
    span = k.shape[0]
    row = lax.broadcasted_iota(jnp.int32, (rows, span), 0)
    col = lax.broadcasted_iota(jnp.int32, (rows, span), 1)
    allowed = (col <= row + (span - rows)) & (kid_ref[...] == qid_ref[...])
    allowed = jnp.concatenate([allowed] * group, axis=0)
    q = jnp.concatenate([q_ref[:, h * HD:(h + 1) * HD] for h in range(group)], axis=0)
    do = jnp.concatenate([do_ref[:, h * HD:(h + 1) * HD] for h in range(group)], axis=0)
    s = lax.dot_general(q, k, (((1,), (1,)), ((), ())), preferred_element_type=jnp.float32) * inverse
    s = jnp.where(allowed, s, NEGATIVE)
    e = jnp.exp(s - jnp.max(s, axis=1, keepdims=True))
    p = e / jnp.sum(e, axis=1, keepdims=True)
    ph = p.astype(jnp.bfloat16)
    oh = jnp.dot(ph, v, preferred_element_type=jnp.float32).astype(jnp.bfloat16)
    delta = jnp.sum(do.astype(jnp.float32) * oh.astype(jnp.float32), axis=1, keepdims=True)
    dp = lax.dot_general(do, v, (((1,), (1,)), ((), ())), preferred_element_type=jnp.float32)
    ds = (p * (dp - delta)).astype(jnp.bfloat16)
    dq = (jnp.dot(ds, k, preferred_element_type=jnp.float32) * inverse).astype(jnp.bfloat16)
    for h in range(group):
        o_ref[:, h * HD:(h + 1) * HD] = oh[h * rows:(h + 1) * rows]
        dq_ref[:, h * HD:(h + 1) * HD] = dq[h * rows:(h + 1) * rows]
    dk_ref[...] = lax.dot_general(ds, q, (((0,), (0,)), ((), ())), preferred_element_type=jnp.float32) * inverse
    dv_ref[...] = lax.dot_general(ph, do, (((0,), (0,)), ((), ())), preferred_element_type=jnp.float32)


def attention(query_ids, key_ids, queries, out_grad, window_blocks, heads_kv):
    rows, width = queries.shape
    blocks = len(window_blocks)
    span = blocks * rows
    group = width // (heads_kv * HD)
    kernel = functools.partial(attn_kernel, group=group, inverse=1.0 / math.sqrt(HD), blocks=blocks)
    wide = group * HD
    key_specs = [pl.BlockSpec((rows, HD), lambda g: (0, g)) for _ in range(blocks)]
    value_specs = [pl.BlockSpec((rows, HD), lambda g: (0, heads_kv + g)) for _ in range(blocks)]
    return pl.pallas_call(
        kernel,
        grid=(heads_kv,),
        in_specs=[
            pl.BlockSpec((rows, 1), lambda g: (0, 0)),
            pl.BlockSpec((1, span), lambda g: (0, 0)),
            pl.BlockSpec((rows, wide), lambda g: (0, g)),
            pl.BlockSpec((rows, wide), lambda g: (0, g)),
        ]
        + key_specs
        + value_specs,
        out_specs=[
            pl.BlockSpec((rows, wide), lambda g: (0, g)),
            pl.BlockSpec((rows, wide), lambda g: (0, g)),
            pl.BlockSpec((span, HD), lambda g: (0, g)),
            pl.BlockSpec((span, HD), lambda g: (0, g)),
        ],
        out_shape=[
            jax.ShapeDtypeStruct((rows, width), jnp.bfloat16),
            jax.ShapeDtypeStruct((rows, width), jnp.bfloat16),
            jax.ShapeDtypeStruct((span, heads_kv * HD), jnp.float32),
            jax.ShapeDtypeStruct((span, heads_kv * HD), jnp.float32),
        ],
        compiler_params=pltpu.CompilerParams(vmem_limit_bytes=56 * 1024 * 1024),
    )(query_ids.reshape(rows, 1), key_ids.reshape(1, span), queries, out_grad, *window_blocks, *window_blocks)


def make_shards(n_data, n_cz, n_cw):
    n_context = n_cz * n_cw

    def shards(queries, keys, values, out_grad, layer_input, doc_lens):
        tok_rows = queries.shape[1]
        kv_width = keys.shape[2]
        heads_kv = kv_width // HD
        group = queries.shape[2] // kv_width
        inverse = 1.0 / math.sqrt(HD)
        blocks_back = min(8, n_context // 4)

        owned = D // (n_data * n_context)

        own_pair = jnp.concatenate([keys[0], values[0]], axis=1)
        earlier = [shifted(own_pair, d, n_context) for d in range(blocks_back, 0, -1)]
        window_blocks = earlier + [own_pair]
        member = lax.axis_index("cw")
        chunks = layer_input[0].reshape(tok_rows, n_data, n_cz, n_cw, owned)
        chunks, window_blocks = lax.optimization_barrier((chunks, window_blocks))
        chunks = chunks.transpose(3, 0, 2, 1, 4).reshape(n_cw, tok_rows, n_cz * n_data * owned)
        received = [lax.dynamic_index_in_dim(chunks, member, 0, keepdims=False)]
        for k in range(1, n_cw):
            route = [(i, (i + k) % n_cw) for i in range(n_cw)]
            outgoing = lax.dynamic_index_in_dim(chunks, (member + k) % n_cw, 0, keepdims=False)
            received.append(lax.ppermute(outgoing, "cw", route))
        column_share = jnp.concatenate(received[::-1], axis=0)
        span = len(window_blocks) * tok_rows
        device = lax.axis_index("cz") * n_cw + lax.axis_index("cw")
        query_pos = device * tok_rows + jnp.arange(tok_rows, dtype=jnp.int32)
        key_pos = (device - blocks_back) * tok_rows + jnp.arange(span, dtype=jnp.int32)
        query_ids = doc_index(doc_lens[0], query_pos)
        key_ids = jnp.where(key_pos >= 0, doc_index(doc_lens[0], key_pos), -1)
        out_half, query_part, key_part, value_part = attention(
            query_ids, key_ids, queries[0], out_grad[0], window_blocks, heads_kv
        )
        grad_scale = 1.0 / math.sqrt(tok_rows * n_context * n_data)

        pair_grad = jnp.concatenate([key_part, value_part], axis=1)

        def block_back(distance):
            first_row = (blocks_back - distance) * tok_rows
            return pair_grad[first_row : first_row + tok_rows]

        total = block_back(0)
        for distance in range(1, blocks_back + 1):
            sent = block_back(distance).astype(jnp.bfloat16)
            total = total + shifted(sent, -distance, n_context).astype(jnp.float32)
        pair_half = total.astype(jnp.bfloat16)
        gathered = [pair_half]
        for k in range(1, n_cw):
            route = [(i, (i + k) % n_cw) for i in range(n_cw)]
            gathered.append(lax.ppermute(pair_half, "cw", route))
        group_grad = jnp.concatenate(gathered[::-1], axis=0)
        batch_grad = lax.dot_general(
            column_share,
            group_grad,
            (((0,), (0,)), ((), ())),
            preferred_element_type=jnp.float32,
        )
        by_layer = lax.psum_scatter(batch_grad * grad_scale, "cz", scatter_dimension=0, tiled=True)
        weight_grad = lax.psum_scatter(by_layer, "dp", scatter_dimension=0, tiled=True)
        attn_out = out_half[None]
        query_grad = query_part[None]
        key_grad = pair_half[:, :kv_width][None]
        value_grad = pair_half[:, kv_width:][None]
        return (attn_out, query_grad, key_grad, value_grad, weight_grad)

    return shards


def solution(mesh):
    n_data = mesh.shape["dp"]
    n_context = mesh.shape["ctx"]
    n_cw = 8 if n_context % 8 == 0 else n_context
    n_cz = n_context // n_cw
    split = Mesh(mesh.devices.reshape(n_data, n_cz, n_cw), ("dp", "cz", "cw"))
    tokens = P("dp", CTX, None)
    in_specs = (tokens, tokens, tokens, tokens, tokens, P("dp", None))
    out_specs = (tokens, tokens, tokens, tokens, P(("dp", "cz", "cw"), None))
    return jax.shard_map(
        make_shards(n_data, n_cz, n_cw),
        mesh=split,
        in_specs=in_specs,
        out_specs=out_specs,
        check_vma=False,
    )
```
